32 devices in a mesh: ctx: 8 (over y, x, core), fsdp: 4 (over z).
Axes of the slice: x: 2, y: 2, z: 4, core: 2. Of those that a mesh axis runs over, the one named last changes fastest.
Arguments:
- inner: bfloat16 [16384, 8192], P('ctx', 'fsdp'), may hold values from -6 to 6
- proj_weight: bfloat16 [32, 8192], P(None, 'fsdp'), may hold values from -0.0625 to 0.0625
- rates: float32 [8192], P('fsdp'), may hold values from 3.0517578e-06 to 0.0333333333
- keep: float32 [16384], P('ctx'), may hold values from 0.216 to 1, as said below
- skip: float32 [8192], P('fsdp'), may hold values from 0.5 to 1.5
- upstream: bfloat16 [16384, 8192], P('ctx', 'fsdp'), may hold values from -6 to 6
Outputs:
- input_grad: bfloat16 [16384, 8192], P('ctx', 'fsdp')
- proj_grad: float32 [32, 8192], P(None, 'fsdp')
The draws below stay inside these ranges and needn't reach their ends.
Inputs may be any that keep to these rules, and one draw needn't show every extreme that they name: `keep`: factors on the tokens' decays.
All inputs are finite; a program needn't handle non-finite values.
Results may differ from the reference program's by a relative error of at most 0.0058.
Values sent between devices are 32-bit elements; how exact they have to be, the bound alone decides.
A program may use at most 128 MiB of HBM per device.

```python
import math
import jax
import jax.numpy as jnp
from jax import lax

E = 8192
N = 16
BLK = 256
SEQ = 16384


def draw_rates(key, part):
    keys = jax.random.split(jax.random.fold_in(key, 5), 3)
    slow = jnp.exp(jax.random.uniform(keys[0], (E,), minval=math.log(0.05 / SEQ), maxval=math.log(0.5 / SEQ)))
    fast = jnp.exp(jax.random.uniform(keys[1], (E,), minval=math.log(1.0 / 50.0), maxval=math.log(1.0 / 30.0)))
    picked = jax.random.randint(keys[2], (E,), 0, 2) == 0
    return jnp.where(picked, fast, slow).astype(jnp.float32)


def draw_keep(key, part):
    keys = jax.random.split(jax.random.fold_in(key, 11), 2)
    places = jax.random.randint(keys[0], (3,), 0, SEQ)
    losses = jax.random.uniform(keys[1], (3,), minval=0.6, maxval=0.8)
    positions = jnp.arange(SEQ)
    struck = positions[None, :] == places[:, None]
    return jnp.prod(jnp.where(struck, losses[:, None], 1.0), axis=0).astype(jnp.float32)


def spiked(result, stream_key, source, target, parts, factor):
    def block_of(position):
        return (jnp.arange(result.shape[position]) // (result.shape[position] // parts)).reshape((-1,) + (1,) * (result.ndim - 1 - position))

    near = jax.random.permutation(stream_key, parts)[block_of(target)]
    far = (block_of(target) + parts // 2) % parts
    return jnp.where((block_of(source) == near) | (block_of(source) == far), factor * result, result)


def levels(own_key, dims, cuts, low, largest):
    gain = 1.0
    for position, parts in cuts:
        draws = jax.random.uniform(jax.random.fold_in(jax.random.fold_in(own_key, 6), position), (parts,), jnp.float32, low / len(cuts), largest / len(cuts))
        gain = gain * jnp.repeat(jnp.exp(draws), dims[position] // parts).reshape((-1,) + (1,) * (len(dims) - 1 - position))
    return gain


def centred(key, extent, width, limit, shards=(), kind=jnp.bfloat16):
    entries = jax.random.normal(key, extent, jnp.float32) * width
    if len(shards) > 0:
        entries = levels(key, extent, shards, -0.22, 0.18) * entries
    return jnp.clip(entries, min=-limit, max=limit).astype(kind)


def heavy_noise(stream_key, dims, spread, reach, shards, heavy, kind=jnp.bfloat16):
    drawn = spread * jax.random.normal(stream_key, dims, jnp.float32)
    if shards:
        drawn = drawn * levels(stream_key, dims, shards, -0.22, 0.18)
    return jnp.clip(spiked(drawn, jax.random.fold_in(stream_key, 3), *heavy), -reach, reach).astype(kind)


def setup_inputs(seed: int = 0) -> dict:
    arg_keys = jax.random.split(jax.random.key(seed), 7)
    inner = centred(arg_keys[0], (SEQ, E), 1.0, 6.0, ((0, 8), (1, 4)))
    proj_weight = centred(arg_keys[1], (2 * N, E), E ** -0.5, 0.0625, ((1, 4),))
    rates = draw_rates(jax.random.fold_in(arg_keys[6], 71), 0)
    keep = draw_keep(jax.random.fold_in(arg_keys[6], 71), 0)
    skip = jnp.clip(0.5 + 1.0 * jax.random.uniform(arg_keys[4], (E,), jnp.float32) ** levels(arg_keys[4], (E,), ((0, 4),), -0.2, 0.2), 0.5, 1.5)
    upstream = heavy_noise(arg_keys[5], (SEQ, E), 1.0, 6.0, ((0, 8), (1, 4)), (0, 1, 8, 2.0))
    return dict(inner=inner, proj_weight=proj_weight, rates=rates, keep=keep, skip=skip, upstream=upstream)


def reference(inner, proj_weight, rates, keep, skip, upstream):
    highest = lax.Precision.HIGHEST

    def mixed(left, right):
        return jnp.dot(left, right, preferred_element_type=jnp.float32)

    def precise(left, right):
        return jnp.dot(left, right, precision=highest)
    factor = 1.0 / jnp.sqrt(jnp.float32(N))
    input_scale = jnp.sqrt(-jnp.expm1(-2.0 * rates))
    offsets = jnp.arange(1, BLK + 1).astype(jnp.float32)
    within_base = jnp.exp(-offsets[:, None] * rates[None, :])
    lower_mask = jnp.tril(jnp.ones((BLK, BLK), dtype=bool))
    coeffs = jnp.dot(inner, proj_weight.T, preferred_element_type=jnp.float32)
    coef_b = coeffs.astype(jnp.bfloat16)
    nblocks = SEQ // BLK
    blocks = (inner.reshape(nblocks, BLK, E), coef_b.reshape(nblocks, BLK, 2 * N), keep.reshape(nblocks, BLK), upstream.reshape(nblocks, BLK, E), coeffs.reshape(nblocks, BLK, 2 * N))

    def prepare(block):
        vals, coef, factors, grads, coef_wide = block
        within = within_base * jnp.cumprod(factors)[:, None]
        scaled = (input_scale[None, :] * vals.astype(jnp.float32) / within).astype(jnp.bfloat16)
        weighted = (within * grads.astype(jnp.float32)).astype(jnp.bfloat16)
        return (coef[:, :N], coef[:, N:], within, scaled, weighted)

    def forward(state, block):
        write_coef, read_coef, within, scaled, weighted = prepare(block)
        new_state = within[-1][None, :] * state + within[-1][None, :] * mixed(write_coef.T, scaled)
        return (new_state, state)

    def backward(adjoint, block):
        write_coef, read_coef, within, scaled, weighted = prepare(block)
        new_adjoint = factor * mixed(read_coef.T, weighted) + within[-1][None, :] * adjoint
        return (new_adjoint, adjoint)
    zero_state = jnp.zeros((N, E), jnp.float32)
    _, state_at = lax.scan(forward, zero_state, blocks)
    _, adjoint_at = lax.scan(backward, zero_state, blocks, reverse=True)

    def finish(accum, item):
        block, state_in, adjoint = item
        write_coef, read_coef, within, scaled, weighted = prepare(block)
        grads = block[3].astype(jnp.float32)
        coef_wide = block[4]
        carried = (within[-1][None, :] * adjoint).astype(jnp.bfloat16)
        state_b = state_in.astype(jnp.bfloat16)
        read_write = jnp.where(lower_mask, mixed(read_coef, write_coef.T), 0.0).astype(jnp.bfloat16)
        grad_cross = jnp.where(lower_mask, mixed(weighted, scaled.T), 0.0)
        scan_grad = input_scale[None, :] / within * (factor * mixed(read_write.T, weighted) + mixed(write_coef, carried))
        write_wide = coef_wide[:, :N]
        read_wide = coef_wide[:, N:]
        grad_write = factor * precise(grad_cross.T, read_wide) + mixed(scaled, carried.T)
        grad_read = factor * (mixed(weighted, state_b.T) + precise(grad_cross, write_wide))
        grad_coef = jnp.concatenate([grad_write, grad_read], axis=1)
        grad_b = grad_coef.astype(jnp.bfloat16)
        back_grad = mixed(grad_b, proj_weight)
        block_grad = (scan_grad + skip[None, :] * grads + back_grad).astype(jnp.bfloat16)
        return (accum + precise(grad_coef.T, block[0].astype(jnp.float32)), block_grad)
    accum, input_grad = lax.scan(finish, jnp.zeros((2 * N, E), jnp.float32), (blocks, state_at, adjoint_at))
    return (input_grad.reshape(SEQ, E), accum / SEQ)
```

```python
import functools

import jax
import jax.numpy as jnp
from jax import lax
from jax.experimental import pallas as pl
from jax.experimental.pallas import tpu as pltpu
from jax.sharding import PartitionSpec as P

BLK = 256
MESH = pl.DeviceIdType.MESH
F32 = jnp.float32
BF16 = jnp.bfloat16


def nt(left, right):
    return lax.dot_general(left, right, (((1,), (1,)), ((), ())), preferred_element_type=F32)


def tn(left, right):
    return lax.dot_general(left, right, (((0,), (0,)), ((), ())), preferred_element_type=F32)


def nn(left, right):
    return jnp.dot(left, right, preferred_element_type=F32)


def split(value):
    high = value.astype(BF16)
    return high, (value - high.astype(F32)).astype(BF16)


def pieces(channels):
    width = 512 if channels % 512 == 0 else channels
    return [slice(at, at + width) for at in range(0, channels, width)]


def one_minus_exp(x):
    series = 1.0 - x / 9.0
    for k in (8.0, 7.0, 6.0, 5.0, 4.0, 3.0, 2.0):
        series = 1.0 - x / k * series
    return jnp.where(x < 0.25, x * series, 1.0 - jnp.exp(-x))


def copy_to(axis, n, me, k, src, dst, sems):
    return pltpu.make_async_remote_copy(
        src_ref=src,
        dst_ref=dst,
        send_sem=sems[0].at[k - 1],
        recv_sem=sems[1].at[k - 1],
        device_id={axis: lax.rem(me + k, n)},
        device_id_type=MESH,
    )


def scatters(axis, n, me, part, got, sems):
    return [
        copy_to(axis, n, me, k, part.at[lax.rem(me + k, n)], got.at[k - 1], sems)
        for k in range(1, n)
    ]


def gathers(axis, n, me, total, sems):
    own = total.at[me]
    return [copy_to(axis, n, me, k, own, own, sems) for k in range(1, n)]


class LineSum:
    def __init__(self, n, me, part, came, total, up_send, up_recv, down_send, down_recv):
        half = n // 2
        self.part, self.came, self.total = part, came, total
        self.up_send, self.up_recv = up_send, up_recv
        self.down_send, self.down_recv = down_send, down_recv
        left = me < half
        self.depth = jnp.where(left, me, n - 1 - me)
        self.middle = self.depth == half - 1
        self.outermost = self.depth == 0
        self.slot = jnp.where(self.middle, 1, 0)
        self.inward = jnp.where(left, me + 1, me - 1)
        self.outward = jnp.where(left, me - 1, me + 1)

    def rising(self, k, slot):
        return pltpu.make_async_remote_copy(
            src_ref=self.part.at[k], dst_ref=self.came.at[slot, k],
            send_sem=self.up_send.at[k], recv_sem=self.up_recv.at[slot, k],
            device_id={"fsdp": self.inward}, device_id_type=MESH,
        )

    def falling(self, k):
        return pltpu.make_async_remote_copy(
            src_ref=self.total.at[k], dst_ref=self.total.at[k],
            send_sem=self.down_send.at[k], recv_sem=self.down_recv.at[k],
            device_id={"fsdp": self.outward}, device_id_type=MESH,
        )

    def first(self, k):
        @pl.when(self.outermost)
        def _():
            self.rising(k, self.slot).start()

    def up(self, k):
        @pl.when(jnp.logical_not(self.outermost))
        def _():
            self.rising(k, 0).wait_recv()
            self.part[k] = self.part[k] + self.came[0, k]
            self.rising(k, self.slot).start()

    def meet(self, k):
        @pl.when(self.middle)
        def _():
            self.rising(k, 1).wait_recv()
            self.total[k] = self.part[k] + self.came[1, k]

            @pl.when(jnp.logical_not(self.outermost))
            def _():
                self.falling(k).start()

    def down(self, k):
        @pl.when(jnp.logical_not(self.middle))
        def _():
            self.falling(k).wait_recv()

            @pl.when(jnp.logical_not(self.outermost))
            def _():
                self.falling(k).start()

    def drain(self, k):
        self.rising(k, self.slot).wait_send()

        @pl.when(jnp.logical_not(self.outermost))
        def _():
            self.falling(k).wait_send()


def main_kernel(
    nstate, factor, nblocks, nf, nc,
    inner_hbm, upstream_hbm, weight, keep, rates, skip,
    out, proj_out,
    upstream, scaled, weighted, partial, base16, inverse16, inverse, last_base, reach, recip,
    cross, part, came, coef, gpart, gcame, grad, short,
    states, before, terms, pack, packed, arriving, leaving, home, arrived, adjoint,
    carried_all, proj, ppart, pgot, ptotal,
    in_sem, up_sem, s1, r1, s2, r2, s3, r3, s4, r4, s5, r5, s6, r6, s7, r7, s8, r8,
):
    size = 2 * nstate
    channels = weight.shape[1]
    width = channels // nc
    fill_width = channels // nblocks
    f = lax.axis_index("fsdp")
    c = lax.axis_index("ctx")
    cols_of = pieces(channels)
    coef_sum = LineSum(nf, f, part, came, coef, s1, r1, s2, r2)
    grad_sum = LineSum(nf, f, gpart, gcame, grad, s5, r5, s6, r6)

    def rows(j):
        return pl.ds(pl.multiple_of(j * BLK, BLK), BLK)

    def fetch_inner(j):
        return pltpu.make_async_copy(inner_hbm.at[rows(j)], out.at[rows(j)], in_sem.at[j])

    def fetch_upstream(j):
        return pltpu.make_async_copy(upstream_hbm.at[rows(j)], upstream.at[rows(j)], up_sem.at[j])

    for j in range(nblocks):
        fetch_inner(j).start()

    barrier = pltpu.get_barrier_semaphore()
    pl.semaphore_signal(barrier, inc=1, device_id={"fsdp": coef_sum.inward}, device_id_type=MESH)

    @pl.when(jnp.logical_not(coef_sum.outermost))
    def _():
        pl.semaphore_signal(barrier, inc=1, device_id={"fsdp": coef_sum.outward}, device_id_type=MESH)

    for k in range(1, nc):
        pl.semaphore_signal(
            barrier, inc=1, device_id={"ctx": lax.rem(c + k, nc)}, device_id_type=MESH
        )

    prod = jnp.concatenate([keep[:, j * BLK : (j + 1) * BLK] for j in range(nblocks)], axis=0)
    lane = lax.broadcasted_iota(jnp.int32, prod.shape, 1)
    shift = 1
    while shift < BLK:
        prod = prod * jnp.where(lane >= shift, pltpu.roll(prod, shift, 1), 1.0)
        shift *= 2
    inverted = 1.0 / prod
    for j in range(nblocks):
        reach[j] = prod[j : j + 1]
        recip[j] = inverted[j : j + 1]
    last_base[...] = jnp.exp(-float(BLK) * rates[...])

    def first_pass(j):
        fetch_upstream(j).start()
        cols = pl.ds(pl.multiple_of(j * fill_width, fill_width), fill_width)
        rate = rates[:, cols]
        gain = jnp.sqrt(one_minus_exp(2.0 * rate))
        offsets = lax.broadcasted_iota(jnp.int32, (BLK, fill_width), 0).astype(F32) + 1.0
        exponent = offsets * rate
        base16[:, cols] = jnp.exp(-exponent).astype(BF16)
        table = gain * jnp.exp(exponent)
        inverse[:, cols] = table
        inverse16[:, cols] = table.astype(BF16)
        fetch_inner(j).wait()
        part[j] = nt(weight[...], out[rows(j), :])

    first_pass(0)
    pl.semaphore_wait(barrier, nc + jnp.where(coef_sum.outermost, 0, 1))
    coef_sum.first(0)

    def first_step(j, carry):
        first_pass(j)
        coef_sum.first(j)
        return carry

    lax.fori_loop(1, nblocks, first_step, 0)

    row = lax.broadcasted_iota(jnp.int32, (BLK, BLK), 0)
    col = lax.broadcasted_iota(jnp.int32, (BLK, BLK), 1)

    def cross_step(j, carry):
        coef_sum.up(j)

        @pl.when(j >= 2)
        def _():
            coef_sum.meet(j - 2)

        @pl.when(j >= 4)
        def _():
            coef_sum.down(j - 4)

        fetch_upstream(j).wait()
        total = jnp.zeros((BLK, BLK), F32)
        for cols in cols_of:
            w = upstream[rows(j), cols] * base16[:, cols]
            s = out[rows(j), cols] * inverse16[:, cols]
            weighted[rows(j), cols] = w
            scaled[rows(j), cols] = s
            total = total + nt(w, s)
        cross[j] = jnp.where(row >= col, total, 0.0)
        return carry

    lax.fori_loop(0, nblocks, cross_step, 0)

    for k in range(nblocks - 2, nblocks):
        coef_sum.meet(k)

    pack[:size] = jnp.zeros_like(pack[:size])
    pack[size:] = jnp.ones_like(pack[size:])

    def state_step(j, carry):
        @pl.when(j >= nblocks - 4)
        def _():
            coef_sum.down(j)

        rounded = coef[j].astype(BF16).astype(F32)
        write = (rounded[:nstate] * recip[j]).astype(BF16)
        read = (rounded[nstate:] * reach[j]).astype(BF16)
        short[j, :nstate] = write
        short[j, nstate:] = read
        for cols in cols_of:
            decay = last_base[:, cols] * reach[j, :, BLK - 1 :]
            state = pack[:nstate, cols]
            sofar = pack[size:, cols]
            term = factor * nn(read, weighted[rows(j), cols])
            states[j, :, cols] = state
            before[j, :, cols] = sofar[:1]
            terms[j, :, cols] = term
            pack[:nstate, cols] = decay * (state + nn(write, scaled[rows(j), cols]))
            pack[nstate:size, cols] = pack[nstate:size, cols] + sofar[:1] * term
            pack[size:, cols] = sofar * decay
        return carry

    lax.fori_loop(0, nblocks, state_step, 0)
    for d in range(nc):
        packed[d] = pack[:, d * width : (d + 1) * width]
    there = [
        copy_to("ctx", nc, c, k, packed.at[lax.rem(c + k, nc)], arriving.at[c], (s3, r3))
        for k in range(1, nc)
    ]
    for copy in there:
        copy.start()
    arriving[c] = packed[c]

    def product_step(j, carry):
        wide = coef[j]
        write = wide[:nstate] * recip[j]
        read = wide[nstate:] * reach[j]
        high, low = split(cross[j])
        both = jnp.concatenate(split(read), axis=0)
        sums = nn(both, high)
        gpart[j, :nstate] = (factor * recip[j]) * (
            sums[:nstate] + (sums[nstate:] + nn(both[:nstate], low))
        )
        both = jnp.concatenate(split(write), axis=0)
        sums = nt(both, high)
        gpart[j, nstate:] = (factor * reach[j]) * (
            sums[:nstate] + (sums[nstate:] + nt(both[:nstate], low))
        )
        return carry

    def near_step(j, carry):
        turned = jnp.where(
            col >= row, factor * tn(short[j, :nstate], short[j, nstate:]), 0.0
        ).astype(BF16)
        for cols in cols_of:
            mixed = nn(turned, weighted[rows(j), cols])
            partial[rows(j), cols] = inverse[:, cols] * mixed + skip[:, cols] * upstream[
                rows(j), cols
            ].astype(F32)
        return carry

    lax.fori_loop(0, nblocks, product_step, 0)
    lax.fori_loop(0, nblocks // 2, near_step, 0)
    for copy in there:
        copy.wait()
    state = jnp.zeros((nstate, width), F32)
    later = state
    for k in range(nc):
        leaving[k, :nstate] = state
        state = arriving[k, :nstate] + arriving[k, size : size + 1] * state
        j = nc - 1 - k
        leaving[j, nstate:] = later
        later = arriving[j, nstate:size] + arriving[j, size : size + 1] * later
    back = [
        copy_to("ctx", nc, c, k, leaving.at[lax.rem(c + k, nc)], home.at[c], (s4, r4))
        for k in range(1, nc)
    ]
    for copy in back:
        copy.start()
    home[c] = leaving[c]
    lax.fori_loop(nblocks // 2, nblocks, near_step, 0)
    for copy in back:
        copy.wait()
    for d in range(nc):
        arrived[:, d * width : (d + 1) * width] = home[d]
    adjoint[...] = arrived[nstate:]

    final_block = nblocks - 1

    def grad_step(k, carry):
        j = final_block - k

        @pl.when(k >= 2)
        def _():
            grad_sum.up(j + 2)

        @pl.when(k >= 5)
        def _():
            grad_sum.meet(j + 5)

        write_part = jnp.zeros((nstate, BLK), F32)
        read_part = jnp.zeros((nstate, BLK), F32)
        for cols in cols_of:
            later = last_base[:, cols] * reach[j, :, BLK - 1 :] * adjoint[:, cols]
            carried = later.astype(BF16)
            adjoint[:, cols] = terms[j, :, cols] + later
            carried_all[j, :, cols] = carried
            state = states[j, :, cols] + before[j, :, cols] * arrived[:nstate, cols]
            write_part = write_part + nt(carried, scaled[rows(j), cols])
            read_part = read_part + nt(state.astype(BF16), weighted[rows(j), cols])
        gpart[j, :nstate] = gpart[j, :nstate] + recip[j] * write_part
        gpart[j, nstate:] = gpart[j, nstate:] + (factor * reach[j]) * read_part
        grad_sum.first(j)
        return carry

    lax.fori_loop(0, nblocks, grad_step, 0)
    grad_sum.up(1)
    grad_sum.meet(5 - 1)
    grad_sum.up(0)
    grad_sum.meet(5 - 2)
    proj[...] = jnp.zeros_like(proj)

    def proj_step(k, carry):
        j = final_block - k

        @pl.when(k < 3)
        def _():
            grad_sum.meet(2 - k)

        grad_sum.down(j)
        stack = jnp.concatenate(split(grad[j]), axis=0)
        for cols in cols_of:
            both = nn(stack, out[rows(j), cols])
            proj[:, cols] = proj[:, cols] + (both[:size] + both[size:])
        return carry

    lax.fori_loop(0, nblocks, proj_step, 0)

    for d in range(nc):
        ppart[d] = proj[:, d * width : (d + 1) * width]
    spread = scatters("ctx", nc, c, ppart, pgot, (s7, r7))
    for copy in spread:
        copy.start()

    def far_step(j, carry):
        high = grad[j].astype(BF16)
        write = short[j, :nstate]
        for cols in cols_of:
            value = partial[rows(j), cols] + inverse[:, cols] * tn(write, carried_all[j, :, cols])
            value = value + tn(high, weight[:, cols])
            out[rows(j), cols] = value.astype(BF16)
        return carry

    lax.fori_loop(0, nblocks // 2, far_step, 0)
    acc = ppart[c]
    for k, copy in enumerate(spread):
        copy.wait()
        acc = acc + pgot[k]
    ptotal[c] = acc
    gathered = gathers("ctx", nc, c, ptotal, (s8, r8))
    for copy in gathered:
        copy.start()
    lax.fori_loop(nblocks // 2, nblocks, far_step, 0)

    def drain_step(k, carry):
        coef_sum.drain(k)
        grad_sum.drain(k)
        return carry

    lax.fori_loop(0, nblocks, drain_step, 0)
    for copy in gathered:
        copy.wait()
    for d in range(nc):
        proj_out[:, d * width : (d + 1) * width] = ptotal[d] / (nblocks * BLK * nc)


def place_kernel(nblocks, source, proj_source, target, proj_target, sems):
    copies = [
        pltpu.make_async_copy(
            source.at[pl.ds(j * BLK, BLK)], target.at[pl.ds(j * BLK, BLK)], sems.at[j]
        )
        for j in range(nblocks)
    ]
    copies.append(pltpu.make_async_copy(proj_source, proj_target, sems.at[nblocks]))
    for copy in copies:
        copy.start()
    for copy in copies:
        copy.wait()


def local(inner, proj_weight, rates, keep, skip, upstream):
    length, channels = inner.shape
    nstate = proj_weight.shape[0] // 2
    size = 2 * nstate
    nblocks = length // BLK
    factor = 1.0 / nstate**0.5
    nf, nc = lax.axis_size("fsdp"), lax.axis_size("ctx")
    whole = pl.BlockSpec(memory_space=pltpu.VMEM)
    anywhere = pl.BlockSpec(memory_space=pl.ANY)
    shape = jax.ShapeDtypeStruct
    width = channels // nc
    vmem, dma = pltpu.VMEM, pltpu.SemaphoreType.DMA
    entry = (nblocks, nstate, channels)
    coefs = (nblocks, size, BLK)
    line = [vmem(coefs, F32), vmem((2, *coefs), F32), vmem(coefs, F32)]
    line_sems = [dma((nblocks,)), dma((2, nblocks)), dma((nblocks,)), dma((nblocks,))]
    peers = [dma((nc - 1,))] * 2
    scratch = (
        [vmem((length, channels), BF16)] * 3
        + [vmem((length, channels), F32)]
        + [vmem((BLK, channels), BF16)] * 2
        + [vmem((BLK, channels), F32), vmem((1, channels), F32)]
        + [vmem((nblocks, 1, BLK), F32)] * 2
        + [vmem((nblocks, BLK, BLK), F32)]
        + line + line + [vmem(coefs, BF16)]
        + [vmem(entry, F32), vmem((nblocks, 1, channels), F32), vmem(entry, F32)]
        + [vmem((size + 8, channels), F32)]
        + [vmem((nc, size + 8, width), F32)] * 2
        + [vmem((nc, size, width), F32)] * 2
        + [vmem((size, channels), F32), vmem((nstate, channels), F32)]
        + [vmem(entry, BF16), vmem((size, channels), F32)]
        + [vmem((nc, size, width), F32), vmem((nc - 1, size, width), F32)]
        + [vmem((nc, size, width), F32)]
        + [dma((nblocks,))] * 2
        + line_sems + peers + peers + line_sems + peers + peers
    )
    made = pl.pallas_call(
        functools.partial(main_kernel, nstate, factor, nblocks, nf, nc),
        in_specs=[anywhere, anywhere, whole, whole, whole, whole],
        out_specs=[whole, whole],
        out_shape=[pltpu.VMEM((length, channels), BF16), pltpu.VMEM((size, channels), F32)],
        scratch_shapes=scratch,
        compiler_params=pltpu.CompilerParams(
            vmem_limit_bytes=55 * 2**20, collective_id=0, has_side_effects=True
        ),
    )(inner, upstream, proj_weight, keep[None], rates[None], skip[None])
    return pl.pallas_call(
        functools.partial(place_kernel, nblocks),
        in_specs=[whole, whole],
        out_specs=[anywhere, anywhere],
        out_shape=[shape((length, channels), BF16), shape((size, channels), F32)],
        scratch_shapes=[dma((nblocks + 1,))],
        compiler_params=pltpu.CompilerParams(vmem_limit_bytes=2**20),
    )(*made)


def solution(mesh):
    placed = (P("ctx", "fsdp"), P(None, "fsdp"), P("fsdp"), P("ctx"), P("fsdp"), P("ctx", "fsdp"))
    return jax.shard_map(
        local,
        mesh=mesh,
        in_specs=placed,
        out_specs=(P("ctx", "fsdp"), P(None, "fsdp")),
        check_vma=False,
    )
```

```python
import functools

import jax
import jax.numpy as jnp
from jax import lax
from jax.experimental import pallas as pl
from jax.experimental.pallas import tpu as pltpu
from jax.sharding import PartitionSpec as P

BLK = 256
LAG = 4
MESH = pl.DeviceIdType.MESH
F32 = jnp.float32
BF16 = jnp.bfloat16


def nt(left, right):
    return lax.dot_general(left, right, (((1,), (1,)), ((), ())), preferred_element_type=F32)


def tn(left, right):
    return lax.dot_general(left, right, (((0,), (0,)), ((), ())), preferred_element_type=F32)


def nn(left, right):
    return jnp.dot(left, right, preferred_element_type=F32)


def split(value):
    high = value.astype(BF16)
    return high, (value - high.astype(F32)).astype(BF16)


def pieces(channels):
    half = channels // 2
    width = 512 if half % 512 == 0 else half
    return [
        (slice(at, at + width), at // half, slice(at % half, at % half + width))
        for at in range(0, channels, width)
    ]


def one_minus_exp(x):
    series = 1.0 - x / 9.0
    for k in (8.0, 7.0, 6.0, 5.0, 4.0, 3.0, 2.0):
        series = 1.0 - x / k * series
    return jnp.where(x < 0.25, x * series, 1.0 - jnp.exp(-x))


def copy_to(axis, n, me, k, src, dst, sems):
    return pltpu.make_async_remote_copy(
        src_ref=src,
        dst_ref=dst,
        send_sem=sems[0].at[k - 1],
        recv_sem=sems[1].at[k - 1],
        device_id={axis: lax.rem(me + k, n)},
        device_id_type=MESH,
    )


def scatters(axis, n, me, part, got, sems):
    return [
        copy_to(axis, n, me, k, part.at[lax.rem(me + k, n)], got.at[k - 1], sems)
        for k in range(1, n)
    ]


def gathers(axis, n, me, total, sems):
    own = total.at[me]
    return [copy_to(axis, n, me, k, own, own, sems) for k in range(1, n)]


class LineSum:
    def __init__(self, n, me, part, came, total, up_send, up_recv, down_send, down_recv):
        half = n // 2
        self.part, self.came, self.total = part, came, total
        self.up_send, self.up_recv = up_send, up_recv
        self.down_send, self.down_recv = down_send, down_recv
        left = me < half
        self.depth = jnp.where(left, me, n - 1 - me)
        self.middle = self.depth == half - 1
        self.outermost = self.depth == 0
        self.slot = jnp.where(self.middle, 1, 0)
        self.inward = jnp.where(left, me + 1, me - 1)
        self.outward = jnp.where(left, me - 1, me + 1)

    def rising(self, k, slot):
        return pltpu.make_async_remote_copy(
            src_ref=self.part.at[k], dst_ref=self.came.at[slot, k],
            send_sem=self.up_send.at[k], recv_sem=self.up_recv.at[slot, k],
            device_id={"fsdp": self.inward}, device_id_type=MESH,
        )

    def falling(self, k):
        return pltpu.make_async_remote_copy(
            src_ref=self.total.at[k], dst_ref=self.total.at[k],
            send_sem=self.down_send.at[k], recv_sem=self.down_recv.at[k],
            device_id={"fsdp": self.outward}, device_id_type=MESH,
        )

    def first(self, k):
        @pl.when(self.outermost)
        def _():
            self.rising(k, self.slot).start()

    def up(self, k):
        @pl.when(jnp.logical_not(self.outermost))
        def _():
            self.rising(k, 0).wait_recv()
            self.part[k] = self.part[k] + self.came[0, k]
            self.rising(k, self.slot).start()

    def meet(self, k):
        @pl.when(self.middle)
        def _():
            self.rising(k, 1).wait_recv()
            self.total[k] = self.part[k] + self.came[1, k]

            @pl.when(jnp.logical_not(self.outermost))
            def _():
                self.falling(k).start()

    def down(self, k):
        @pl.when(jnp.logical_not(self.middle))
        def _():
            self.falling(k).wait_recv()

            @pl.when(jnp.logical_not(self.outermost))
            def _():
                self.falling(k).start()

    def drain(self, k):
        self.rising(k, self.slot).wait_send()

        @pl.when(jnp.logical_not(self.outermost))
        def _():
            self.falling(k).wait_send()


def main_kernel(
    nstate, factor, nblocks, nf, nc,
    inner_hbm, upstream_hbm, weight, keep, rates, skip,
    out, proj_out,
    upstream, scaled, weighted, partial, base16, inverse, last_base, reach, recip,
    cross, part, came, coef, gpart, gcame, grad, short,
    states, before, terms, sofar, pack, pairs, chip, chips, leaving, arrived, kept, kept_all,
    carried_all, proj, ppart, pgot, ptotal,
    in_sem, up_sem, pair_sems, back_sems, s0, r0, s1, r1, s2, r2, s3, r3, s5, r5, s6, r6, s7, r7, s8, r8,
):
    size = 2 * nstate
    channels = weight.shape[1]
    length = nblocks * BLK
    half = channels // 2
    width = channels // nc
    nq = nc // 2
    fill_width = channels // nblocks
    f = lax.axis_index("fsdp")
    c = lax.axis_index("ctx")
    q, h = c // 2, lax.rem(c, 2)
    other = 1 - h
    cols_of = pieces(channels)
    coef_sum = LineSum(nf, f, part, came, coef, s1, r1, s2, r2)
    grad_sum = LineSum(nf, f, gpart, gcame, grad, s5, r5, s6, r6)

    def rows(j):
        return pl.ds(pl.multiple_of(j * BLK, BLK), BLK)

    def fetch_inner(j):
        return pltpu.make_async_copy(inner_hbm.at[rows(j)], out.at[rows(j)], in_sem.at[j])

    def fetch_upstream(j):
        return pltpu.make_async_copy(upstream_hbm.at[rows(j)], upstream.at[rows(j)], up_sem.at[j])

    def to_partner(src, dst, sems):
        return pltpu.make_async_remote_copy(
            src_ref=src, dst_ref=dst, send_sem=sems.at[0], recv_sem=sems.at[1],
            device_id={"ctx": 2 * q + other}, device_id_type=MESH,
        )

    def both(step, j):
        step(2 * j)
        step(2 * j + 1)

    for j in range(nblocks):
        fetch_inner(j).start()

    barrier = pltpu.get_barrier_semaphore()
    pl.semaphore_signal(barrier, inc=1, device_id={"fsdp": coef_sum.inward}, device_id_type=MESH)

    @pl.when(jnp.logical_not(coef_sum.outermost))
    def _():
        pl.semaphore_signal(barrier, inc=1, device_id={"fsdp": coef_sum.outward}, device_id_type=MESH)

    for k in range(1, nc):
        pl.semaphore_signal(
            barrier, inc=1, device_id={"ctx": lax.rem(c + k, nc)}, device_id_type=MESH
        )

    prod = jnp.concatenate([keep[:, j * BLK : (j + 1) * BLK] for j in range(nblocks)], axis=0)
    lane = lax.broadcasted_iota(jnp.int32, prod.shape, 1)
    shift = 1
    while shift < BLK:
        prod = prod * jnp.where(lane >= shift, pltpu.roll(prod, shift, 1), 1.0)
        shift *= 2
    inverted = 1.0 / prod
    whole_keep = jnp.ones((1, 1), F32)
    for j in range(nblocks):
        reach[j] = prod[j : j + 1]
        recip[j] = inverted[j : j + 1]
        whole_keep = whole_keep * prod[j : j + 1, BLK - 1 :]
    kept[...] = jnp.broadcast_to(whole_keep, kept.shape)
    kept_all[c] = kept[...]
    last_base[...] = jnp.exp(-float(BLK) * rates[...])

    def first_pass(j):
        cols = pl.ds(pl.multiple_of(j * fill_width, fill_width), fill_width)
        rate = rates[:, cols]
        gain = jnp.sqrt(one_minus_exp(2.0 * rate))
        offsets = lax.broadcasted_iota(jnp.int32, (BLK, fill_width), 0).astype(F32) + 1.0
        exponent = offsets * rate
        base16[:, cols] = jnp.exp(-exponent).astype(BF16)
        inverse[:, cols] = gain * jnp.exp(exponent)
        fetch_inner(j).wait()
        sums = nt(weight[...], out[rows(j), :])
        part[2 * j] = sums[:nstate]
        part[2 * j + 1] = sums[nstate:]

    first_pass(0)
    pl.semaphore_wait(barrier, nc + jnp.where(coef_sum.outermost, 0, 1))
    both(coef_sum.first, 0)
    keeps = [
        copy_to("ctx", nc, c, k, kept, kept_all.at[c], (s0, r0)) for k in range(1, nc)
    ]
    for copy in keeps:
        copy.start()

    def first_step(j, carry):
        @pl.when(j >= nblocks // 2)
        def _():
            fetch_upstream(2 * j - nblocks).start()
            fetch_upstream(2 * j - nblocks + 1).start()

        first_pass(j)
        both(coef_sum.first, j)
        return carry

    lax.fori_loop(1, nblocks, first_step, 0)

    row = lax.broadcasted_iota(jnp.int32, (BLK, BLK), 0)
    col = lax.broadcasted_iota(jnp.int32, (BLK, BLK), 1)

    def cross_step(j, carry):
        both(coef_sum.up, j)

        @pl.when(j >= LAG)
        def _():
            both(coef_sum.meet, j - LAG)

        fetch_upstream(j).wait()
        total = jnp.zeros((BLK, BLK), F32)
        for cols, _, _ in cols_of:
            w = upstream[rows(j), cols] * base16[:, cols]
            s = (out[rows(j), cols].astype(F32) * inverse[:, cols]).astype(BF16)
            weighted[rows(j), cols] = w
            scaled[rows(j), cols] = s
            total = total + nt(w, s)
        cross[j] = jnp.where(row >= col, total, 0.0)
        return carry

    lax.fori_loop(0, nblocks, cross_step, 0)

    pack[...] = jnp.zeros_like(pack)
    sofar[...] = jnp.ones_like(sofar)

    def state_step(j, carry):
        @pl.when(j < LAG)
        def _():
            both(coef_sum.meet, nblocks - LAG + j)

        both(coef_sum.down, j)
        write = (coef[2 * j].astype(BF16).astype(F32) * recip[j]).astype(BF16)
        read = (coef[2 * j + 1].astype(BF16).astype(F32) * reach[j]).astype(BF16)
        short[j, :nstate] = write
        short[j, nstate:] = read
        for cols, part_of, inside in cols_of:
            decay = last_base[:, cols] * reach[j, :, BLK - 1 :]
            state = pack[part_of, :nstate, inside]
            ahead = sofar[:, cols]
            term = factor * nn(read, weighted[rows(j), cols])
            states[j, :, cols] = state
            before[j, :, cols] = ahead
            terms[j, :, cols] = term
            pack[part_of, :nstate, inside] = decay * (state + nn(write, scaled[rows(j), cols]))
            pack[part_of, nstate:, inside] = pack[part_of, nstate:, inside] + ahead * term
            sofar[:, cols] = ahead * decay
        return carry

    lax.fori_loop(0, nblocks, state_step, 0)
    across = to_partner(pack.at[other], pairs.at[h], pair_sems)
    across.start()
    pairs[h] = pack[h]

    def product_step(j, carry):
        write = coef[2 * j] * recip[j]
        read = coef[2 * j + 1] * reach[j]
        high, low = split(cross[j])
        two = jnp.concatenate(split(read), axis=0)
        sums = nn(two, high)
        gpart[2 * j] = (factor * recip[j]) * (
            sums[:nstate] + (sums[nstate:] + nn(two[:nstate], low))
        )
        two = jnp.concatenate(split(write), axis=0)
        sums = nt(two, high)
        gpart[2 * j + 1] = (factor * reach[j]) * (
            sums[:nstate] + (sums[nstate:] + nt(two[:nstate], low))
        )
        return carry

    def near(j):
        turned = jnp.where(
            col >= row, factor * tn(short[j, :nstate], short[j, nstate:]), 0.0
        ).astype(BF16)
        for cols, _, _ in cols_of:
            mixed = nn(turned, weighted[rows(j), cols])
            partial[rows(j), cols] = inverse[:, cols] * mixed + skip[:, cols] * upstream[
                rows(j), cols
            ].astype(F32)

    def near_step(j, carry):
        near(j)
        return carry

    lax.fori_loop(0, nblocks // 4, product_step, 0)
    for copy in keeps:
        copy.wait()
    across.wait()
    span = jnp.exp(-float(length) * rates[:, pl.ds(pl.multiple_of(h * half, half), half)])

    def decay_of(device):
        return span * kept_all[device, :1, :1]

    decay0, decay1 = decay_of(2 * q), decay_of(2 * q + 1)
    chip[0] = pairs[1, :nstate] + decay1 * pairs[0, :nstate]
    chip[1] = pairs[0, nstate:] + decay0 * pairs[1, nstate:]
    there = []
    for k in range(1, nq):
        peer = lax.rem(q + k, nq)
        there.append(
            pltpu.make_async_remote_copy(
                src_ref=chip.at[jnp.where(peer > q, 0, 1)], dst_ref=chips.at[q],
                send_sem=s3.at[k - 1], recv_sem=r3.at[k - 1],
                device_id={"ctx": 2 * peer + h}, device_id_type=MESH,
            )
        )
    for copy in there:
        copy.start()
    lax.fori_loop(nblocks // 4, nblocks, product_step, 0)
    lax.fori_loop(0, nblocks // 2, near_step, 0)
    for copy in there:
        copy.wait()

    def chip_decay(k):
        return decay_of(2 * k) * decay_of(2 * k + 1)

    zero = jnp.zeros((nstate, half), F32)
    state = lax.fori_loop(0, q, lambda k, state: chips[k] + chip_decay(k) * state, zero)
    later = lax.fori_loop(
        0, nq - 1 - q, lambda k, later: chips[nq - 1 - k] + chip_decay(nq - 1 - k) * later, zero
    )
    leaving[0, :nstate] = state
    leaving[0, nstate:] = pairs[1, nstate:] + decay1 * later
    leaving[1, :nstate] = pairs[0, :nstate] + decay0 * state
    leaving[1, nstate:] = later
    home = to_partner(leaving.at[other], arrived.at[h], back_sems)
    home.start()
    arrived[h] = leaving[h]
    home.wait()

    final_block = nblocks - 1

    def grad_step(k, carry):
        j = final_block - k

        @pl.when(k >= LAG)
        def _():
            both(grad_sum.up, j + LAG)

        write_part = jnp.zeros((nstate, BLK), F32)
        read_part = jnp.zeros((nstate, BLK), F32)
        for cols, part_of, inside in cols_of:
            later = last_base[:, cols] * reach[j, :, BLK - 1 :] * arrived[part_of, nstate:, inside]
            carried = later.astype(BF16)
            arrived[part_of, nstate:, inside] = terms[j, :, cols] + later
            carried_all[j, :, cols] = carried
            state = states[j, :, cols] + before[j, :, cols] * arrived[part_of, :nstate, inside]
            write_part = write_part + nt(carried, scaled[rows(j), cols])
            read_part = read_part + nt(state.astype(BF16), weighted[rows(j), cols])
        gpart[2 * j] = gpart[2 * j] + recip[j] * write_part
        gpart[2 * j + 1] = gpart[2 * j + 1] + (factor * reach[j]) * read_part
        both(grad_sum.first, j)
        return carry

    lax.fori_loop(0, nblocks, grad_step, 0)

    def turn_step(k, carry):
        both(grad_sum.up, LAG - 1 - k)
        both(grad_sum.meet, final_block - k)
        near(nblocks // 2 + k)
        return carry

    lax.fori_loop(0, LAG, turn_step, 0)
    proj[...] = jnp.zeros_like(proj)

    def proj_step(k, carry):
        j = final_block - k

        @pl.when(k < nblocks - LAG)
        def _():
            both(grad_sum.meet, j - LAG)

        both(grad_sum.down, j)
        write_high, write_low = split(grad[2 * j])
        read_high, read_low = split(grad[2 * j + 1])
        stack = jnp.concatenate([write_high, read_high, write_low, read_low], axis=0)
        for cols, _, _ in cols_of:
            two = nn(stack, out[rows(j), cols])
            proj[:, cols] = proj[:, cols] + (two[:size] + two[size:])
        return carry

    lax.fori_loop(0, nblocks, proj_step, 0)

    for d in range(nc):
        ppart[d] = proj[:, d * width : (d + 1) * width]
    spread = scatters("ctx", nc, c, ppart, pgot, (s7, r7))
    for copy in spread:
        copy.start()

    def far_step(j, carry):
        high = jnp.concatenate([grad[2 * j].astype(BF16), grad[2 * j + 1].astype(BF16)], axis=0)
        write = short[j, :nstate]
        for cols, _, _ in cols_of:
            value = partial[rows(j), cols] + inverse[:, cols] * tn(write, carried_all[j, :, cols])
            value = value + tn(high, weight[:, cols])
            out[rows(j), cols] = value.astype(BF16)
        return carry

    lax.fori_loop(0, nblocks // 2, far_step, 0)
    acc = ppart[c]
    for k, copy in enumerate(spread):
        copy.wait()
        acc = acc + pgot[k]
    ptotal[c] = acc
    gathered = gathers("ctx", nc, c, ptotal, (s8, r8))
    for copy in gathered:
        copy.start()
    lax.fori_loop(nblocks // 2, nblocks, far_step, 0)

    def drain_step(k, carry):
        coef_sum.drain(k)
        grad_sum.drain(k)
        return carry

    lax.fori_loop(0, 2 * nblocks, drain_step, 0)
    for copy in gathered:
        copy.wait()
    for d in range(nc):
        proj_out[:, d * width : (d + 1) * width] = ptotal[d] / (length * nc)


def place_kernel(nblocks, source, proj_source, target, proj_target, sems):
    copies = [
        pltpu.make_async_copy(
            source.at[pl.ds(j * BLK, BLK)], target.at[pl.ds(j * BLK, BLK)], sems.at[j]
        )
        for j in range(nblocks)
    ]
    copies.append(pltpu.make_async_copy(proj_source, proj_target, sems.at[nblocks]))
    for copy in copies:
        copy.start()
    for copy in copies:
        copy.wait()


def local(inner, proj_weight, rates, keep, skip, upstream):
    length, channels = inner.shape
    nstate = proj_weight.shape[0] // 2
    size = 2 * nstate
    nblocks = length // BLK
    factor = 1.0 / nstate**0.5
    nf, nc = lax.axis_size("fsdp"), lax.axis_size("ctx")
    whole = pl.BlockSpec(memory_space=pltpu.VMEM)
    anywhere = pl.BlockSpec(memory_space=pl.ANY)
    shape = jax.ShapeDtypeStruct
    width = channels // nc
    vmem, dma = pltpu.VMEM, pltpu.SemaphoreType.DMA
    entry = (nblocks, nstate, channels)
    half, nq = channels // 2, nc // 2
    chunks = (2 * nblocks, nstate, BLK)
    line = [vmem(chunks, F32), vmem((2, *chunks), F32), vmem(chunks, F32)]
    line_sems = [dma(chunks[:1]), dma((2, *chunks[:1])), dma(chunks[:1]), dma(chunks[:1])]
    peers = [dma((nc - 1,))] * 2
    scratch = (
        [vmem((length, channels), BF16)] * 3
        + [vmem((length, channels), F32)]
        + [vmem((BLK, channels), BF16)]
        + [vmem((BLK, channels), F32), vmem((1, channels), F32)]
        + [vmem((nblocks, 1, BLK), F32)] * 2
        + [vmem((nblocks, BLK, BLK), F32)]
        + line + line + [vmem((nblocks, size, BLK), BF16)]
        + [vmem(entry, F32), vmem((nblocks, 1, channels), F32), vmem(entry, F32)]
        + [vmem((1, channels), F32)]
        + [vmem((2, size, half), F32)] * 2
        + [vmem((2, nstate, half), F32), vmem((nq, nstate, half), F32)]
        + [vmem((2, size, half), F32)] * 2
        + [vmem((8, 128), F32), vmem((nc, 8, 128), F32)]
        + [vmem(entry, BF16), vmem((size, channels), F32)]
        + [vmem((nc, size, width), F32), vmem((nc - 1, size, width), F32)]
        + [vmem((nc, size, width), F32)]
        + [dma((nblocks,))] * 2
        + [dma((2,))] * 2
        + peers + line_sems + [dma((nq - 1,))] * 2 + line_sems + peers + peers
    )
    made = pl.pallas_call(
        functools.partial(main_kernel, nstate, factor, nblocks, nf, nc),
        in_specs=[anywhere, anywhere, whole, whole, whole, whole],
        out_specs=[whole, whole],
        out_shape=[pltpu.VMEM((length, channels), BF16), pltpu.VMEM((size, channels), F32)],
        scratch_shapes=scratch,
        compiler_params=pltpu.CompilerParams(
            vmem_limit_bytes=55 * 2**20, collective_id=0, has_side_effects=True
        ),
    )(inner, upstream, proj_weight, keep[None], rates[None], skip[None])
    return pl.pallas_call(
        functools.partial(place_kernel, nblocks),
        in_specs=[whole, whole],
        out_specs=[anywhere, anywhere],
        out_shape=[shape((length, channels), BF16), shape((size, channels), F32)],
        scratch_shapes=[dma((nblocks + 1,))],
        compiler_params=pltpu.CompilerParams(vmem_limit_bytes=2**20),
    )(*made)


def solution(mesh):
    placed = (P("ctx", "fsdp"), P(None, "fsdp"), P("fsdp"), P("ctx"), P("fsdp"), P("ctx", "fsdp"))
    return jax.shard_map(
        local,
        mesh=mesh,
        in_specs=placed,
        out_specs=(P("ctx", "fsdp"), P(None, "fsdp")),
        check_vma=False,
    )
```

```python
import functools

import jax
import jax.numpy as jnp
from jax import lax
from jax.experimental import pallas as pl
from jax.experimental.pallas import tpu as pltpu
from jax.sharding import PartitionSpec as P

BLK = 256
LAG = 4
AHEAD = 3
MESH = pl.DeviceIdType.MESH
F32 = jnp.float32
BF16 = jnp.bfloat16


def nt(left, right):
    return lax.dot_general(left, right, (((1,), (1,)), ((), ())), preferred_element_type=F32)


def tn(left, right):
    return lax.dot_general(left, right, (((0,), (0,)), ((), ())), preferred_element_type=F32)


def nn(left, right):
    return jnp.dot(left, right, preferred_element_type=F32)


def split(value):
    high = value.astype(BF16)
    return high, (value - high.astype(F32)).astype(BF16)


def pieces(channels):
    half = channels // 2
    width = 512 if half % 512 == 0 else half
    return [
        (slice(at, at + width), at // half, slice(at % half, at % half + width))
        for at in range(0, channels, width)
    ]


def one_minus_exp(x):
    series = 1.0 - x / 9.0
    for k in (8.0, 7.0, 6.0, 5.0, 4.0, 3.0, 2.0):
        series = 1.0 - x / k * series
    return jnp.where(x < 0.25, x * series, 1.0 - jnp.exp(-x))


def copy_to(axis, n, me, k, src, dst, sems):
    return pltpu.make_async_remote_copy(
        src_ref=src,
        dst_ref=dst,
        send_sem=sems[0].at[k - 1],
        recv_sem=sems[1].at[k - 1],
        device_id={axis: lax.rem(me + k, n)},
        device_id_type=MESH,
    )


def scatters(axis, n, me, part, got, sems):
    return [
        copy_to(axis, n, me, k, part.at[lax.rem(me + k, n)], got.at[k - 1], sems)
        for k in range(1, n)
    ]


def gathers(axis, n, me, total, sems):
    own = total.at[me]
    return [copy_to(axis, n, me, k, own, own, sems) for k in range(1, n)]


class LineSum:
    def __init__(self, n, me, part, came, total, up_send, up_recv, down_send, down_recv):
        half = n // 2
        self.part, self.came, self.total = part, came, total
        self.up_send, self.up_recv = up_send, up_recv
        self.down_send, self.down_recv = down_send, down_recv
        left = me < half
        self.depth = jnp.where(left, me, n - 1 - me)
        self.middle = self.depth == half - 1
        self.outermost = self.depth == 0
        self.slot = jnp.where(self.middle, 1, 0)
        self.inward = jnp.where(left, me + 1, me - 1)
        self.outward = jnp.where(left, me - 1, me + 1)

    def rising(self, k, slot):
        return pltpu.make_async_remote_copy(
            src_ref=self.part.at[k], dst_ref=self.came.at[slot, k],
            send_sem=self.up_send.at[k], recv_sem=self.up_recv.at[slot, k],
            device_id={"fsdp": self.inward}, device_id_type=MESH,
        )

    def falling(self, k):
        return pltpu.make_async_remote_copy(
            src_ref=self.total.at[k], dst_ref=self.total.at[k],
            send_sem=self.down_send.at[k], recv_sem=self.down_recv.at[k],
            device_id={"fsdp": self.outward}, device_id_type=MESH,
        )

    def first(self, k):
        @pl.when(self.outermost)
        def _():
            self.rising(k, self.slot).start()

    def up(self, k):
        @pl.when(jnp.logical_not(self.outermost))
        def _():
            self.rising(k, 0).wait_recv()
            self.part[k] = self.part[k] + self.came[0, k]
            self.rising(k, self.slot).start()

    def meet(self, k):
        @pl.when(self.middle)
        def _():
            self.rising(k, 1).wait_recv()
            self.total[k] = self.part[k] + self.came[1, k]

            @pl.when(jnp.logical_not(self.outermost))
            def _():
                self.falling(k).start()

    def down(self, k):
        @pl.when(jnp.logical_not(self.middle))
        def _():
            self.falling(k).wait_recv()

            @pl.when(jnp.logical_not(self.outermost))
            def _():
                self.falling(k).start()

    def drain(self, k):
        self.rising(k, self.slot).wait_send()

        @pl.when(jnp.logical_not(self.outermost))
        def _():
            self.falling(k).wait_send()


def main_kernel(
    nstate, factor, nblocks, nf, nc,
    inner_hbm, upstream_hbm, weight_hbm, keep_hbm, rates_hbm, skip_hbm,
    out, proj_out,
    weight, keep, rates, skip,
    upstream, scaled, weighted, partial, base16, inverse, last_base, reach, recip,
    cross, part, came, coef, gpart, gcame, grad, short,
    states, before, terms, sofar, pack, pairs, chip, chips, leaving, arrived, kept, kept_all,
    carried_all, proj, ppart, pgot, ptotal,
    small_sem, in_sem, up_sem, pair_sems, back_sems, s0, r0, s1, r1, s2, r2, s3, r3, s5, r5, s6, r6, s7, r7, s8, r8,
):
    size = 2 * nstate
    channels = weight.shape[1]
    length = nblocks * BLK
    half = channels // 2
    width = channels // nc
    nq = nc // 2
    fill_width = channels // nblocks
    f = lax.axis_index("fsdp")
    c = lax.axis_index("ctx")
    q, h = c // 2, lax.rem(c, 2)
    other = 1 - h
    cols_of = pieces(channels)
    coef_sum = LineSum(nf, f, part, came, coef, s1, r1, s2, r2)
    grad_sum = LineSum(nf, f, gpart, gcame, grad, s5, r5, s6, r6)

    def rows(j):
        return pl.ds(pl.multiple_of(j * BLK, BLK), BLK)

    def fetch_inner(j):
        return pltpu.make_async_copy(inner_hbm.at[rows(j)], out.at[rows(j)], in_sem.at[j])

    def fetch_upstream(j):
        return pltpu.make_async_copy(upstream_hbm.at[rows(j)], upstream.at[rows(j)], up_sem.at[j])

    def to_partner(src, dst, sems):
        return pltpu.make_async_remote_copy(
            src_ref=src, dst_ref=dst, send_sem=sems.at[0], recv_sem=sems.at[1],
            device_id={"ctx": 2 * q + other}, device_id_type=MESH,
        )

    small = [
        pltpu.make_async_copy(source, target, small_sem.at[i])
        for i, (source, target) in enumerate(
            ((weight_hbm, weight), (keep_hbm, keep), (rates_hbm, rates), (skip_hbm, skip))
        )
    ]
    small[0].start()
    fetch_inner(0).start()
    for copy in small[1:]:
        copy.start()
    for j in range(1, AHEAD):
        fetch_inner(j).start()

    barrier = pltpu.get_barrier_semaphore()
    pl.semaphore_signal(barrier, inc=1, device_id={"fsdp": coef_sum.inward}, device_id_type=MESH)

    @pl.when(jnp.logical_not(coef_sum.outermost))
    def _():
        pl.semaphore_signal(barrier, inc=1, device_id={"fsdp": coef_sum.outward}, device_id_type=MESH)

    for k in range(1, nc):
        pl.semaphore_signal(
            barrier, inc=1, device_id={"ctx": lax.rem(c + k, nc)}, device_id_type=MESH
        )

    def fill(j):
        cols = pl.ds(pl.multiple_of(j * fill_width, fill_width), fill_width)
        rate = rates[:, cols]
        gain = jnp.sqrt(one_minus_exp(2.0 * rate))
        offsets = lax.broadcasted_iota(jnp.int32, (BLK, fill_width), 0).astype(F32) + 1.0
        exponent = offsets * rate
        base16[:, cols] = jnp.exp(-exponent).astype(BF16)
        inverse[:, cols] = gain * jnp.exp(exponent)

    def first_pass(j):
        sums = nt(weight[...], out[rows(j), :])
        part[j, :nstate] = sums[:nstate]
        part[j, nstate:] = sums[nstate:]

    small[0].wait()

    def first_step(j, carry):
        fetch_inner(j).wait()

        @pl.when(j < nblocks - AHEAD)
        def _():
            fetch_inner(j + AHEAD).start()

        @pl.when(j >= nblocks - AHEAD)
        def _():
            fetch_upstream(j - (nblocks - AHEAD)).start()

        first_pass(j)

        @pl.when(j == 0)
        def _():
            pl.semaphore_wait(barrier, nc + jnp.where(coef_sum.outermost, 0, 1))

        coef_sum.first(j)
        return carry

    lax.fori_loop(0, nblocks, first_step, 0)
    for copy in small[1:]:
        copy.wait()
    prod = jnp.concatenate([keep[:, j * BLK : (j + 1) * BLK] for j in range(nblocks)], axis=0)
    lane = lax.broadcasted_iota(jnp.int32, prod.shape, 1)
    shift = 1
    while shift < BLK:
        prod = prod * jnp.where(lane >= shift, pltpu.roll(prod, shift, 1), 1.0)
        shift *= 2
    inverted = 1.0 / prod
    whole_keep = jnp.ones((1, 1), F32)
    for j in range(nblocks):
        reach[j] = prod[j : j + 1]
        recip[j] = inverted[j : j + 1]
        whole_keep = whole_keep * prod[j : j + 1, BLK - 1 :]
    kept[...] = jnp.broadcast_to(whole_keep, kept.shape)
    kept_all[c] = kept[...]
    last_base[...] = jnp.exp(-float(BLK) * rates[...])

    keeps = [
        copy_to("ctx", nc, c, k, kept, kept_all.at[c], (s0, r0)) for k in range(1, nc)
    ]
    for copy in keeps:
        copy.start()

    def fill_step(j, carry):
        fill(j)
        return carry

    lax.fori_loop(0, nblocks, fill_step, 0)

    row = lax.broadcasted_iota(jnp.int32, (BLK, BLK), 0)
    col = lax.broadcasted_iota(jnp.int32, (BLK, BLK), 1)

    def cross_step(j, carry):
        coef_sum.up(j)

        @pl.when(j >= LAG)
        def _():
            coef_sum.meet(j - LAG)

        fetch_upstream(j).wait()

        @pl.when(j < nblocks - AHEAD)
        def _():
            fetch_upstream(j + AHEAD).start()

        total = jnp.zeros((BLK, BLK), F32)
        for cols, _, _ in cols_of:
            w = upstream[rows(j), cols] * base16[:, cols]
            s = (out[rows(j), cols].astype(F32) * inverse[:, cols]).astype(BF16)
            weighted[rows(j), cols] = w
            scaled[rows(j), cols] = s
            total = total + nt(w, s)
        cross[j] = jnp.where(row >= col, total, 0.0)
        return carry

    lax.fori_loop(0, nblocks, cross_step, 0)

    pack[...] = jnp.zeros_like(pack)
    sofar[...] = jnp.ones_like(sofar)

    def state_step(j, carry):
        @pl.when(j < LAG)
        def _():
            coef_sum.meet(nblocks - LAG + j)

        coef_sum.down(j)
        write = (coef[j, :nstate].astype(BF16).astype(F32) * recip[j]).astype(BF16)
        read = (coef[j, nstate:].astype(BF16).astype(F32) * reach[j]).astype(BF16)
        short[j, :nstate] = write
        short[j, nstate:] = read
        for cols, part_of, inside in cols_of:
            decay = last_base[:, cols] * reach[j, :, BLK - 1 :]
            state = pack[part_of, :nstate, inside]
            ahead = sofar[:, cols]
            term = factor * nn(read, weighted[rows(j), cols])
            states[j, :, cols] = state
            before[j, :, cols] = ahead
            terms[j, :, cols] = term
            pack[part_of, :nstate, inside] = decay * (state + nn(write, scaled[rows(j), cols]))
            pack[part_of, nstate:, inside] = pack[part_of, nstate:, inside] + ahead * term
            sofar[:, cols] = ahead * decay
        return carry

    lax.fori_loop(0, nblocks, state_step, 0)
    across = to_partner(pack.at[other], pairs.at[h], pair_sems)
    across.start()
    pairs[h] = pack[h]

    def product_step(j, carry):
        write = coef[j, :nstate] * recip[j]
        read = coef[j, nstate:] * reach[j]
        high, low = split(cross[j])
        two = jnp.concatenate(split(read), axis=0)
        sums = nn(two, high)
        gpart[j, :nstate] = (factor * recip[j]) * (
            sums[:nstate] + (sums[nstate:] + nn(two[:nstate], low))
        )
        two = jnp.concatenate(split(write), axis=0)
        sums = nt(two, high)
        gpart[j, nstate:] = (factor * reach[j]) * (
            sums[:nstate] + (sums[nstate:] + nt(two[:nstate], low))
        )
        return carry

    def near(j):
        turned = jnp.where(
            col >= row, factor * tn(short[j, :nstate], short[j, nstate:]), 0.0
        ).astype(BF16)
        for cols, _, _ in cols_of:
            mixed = nn(turned, weighted[rows(j), cols])
            partial[rows(j), cols] = inverse[:, cols] * mixed + skip[:, cols] * upstream[
                rows(j), cols
            ].astype(F32)

    def near_step(j, carry):
        near(j)
        return carry

    lax.fori_loop(0, nblocks // 4, product_step, 0)
    for copy in keeps:
        copy.wait()
    across.wait()
    span = jnp.exp(-float(length) * rates[:, pl.ds(pl.multiple_of(h * half, half), half)])

    def decay_of(device):
        return span * kept_all[device, :1, :1]

    decay0, decay1 = decay_of(2 * q), decay_of(2 * q + 1)
    chip[0] = pairs[1, :nstate] + decay1 * pairs[0, :nstate]
    chip[1] = pairs[0, nstate:] + decay0 * pairs[1, nstate:]
    there = []
    for k in range(1, nq):
        peer = lax.rem(q + k, nq)
        there.append(
            pltpu.make_async_remote_copy(
                src_ref=chip.at[jnp.where(peer > q, 0, 1)], dst_ref=chips.at[q],
                send_sem=s3.at[k - 1], recv_sem=r3.at[k - 1],
                device_id={"ctx": 2 * peer + h}, device_id_type=MESH,
            )
        )
    for copy in there:
        copy.start()
    lax.fori_loop(nblocks // 4, nblocks, product_step, 0)
    lax.fori_loop(0, nblocks // 2, near_step, 0)
    for copy in there:
        copy.wait()

    def chip_decay(k):
        return decay_of(2 * k) * decay_of(2 * k + 1)

    zero = jnp.zeros((nstate, half), F32)
    state = lax.fori_loop(0, q, lambda k, state: chips[k] + chip_decay(k) * state, zero)
    later = lax.fori_loop(
        0, nq - 1 - q, lambda k, later: chips[nq - 1 - k] + chip_decay(nq - 1 - k) * later, zero
    )
    leaving[0, :nstate] = state
    leaving[0, nstate:] = pairs[1, nstate:] + decay1 * later
    leaving[1, :nstate] = pairs[0, :nstate] + decay0 * state
    leaving[1, nstate:] = later
    home = to_partner(leaving.at[other], arrived.at[h], back_sems)
    home.start()
    arrived[h] = leaving[h]
    home.wait()

    final_block = nblocks - 1

    def grad_step(k, carry):
        j = final_block - k

        @pl.when(k >= LAG)
        def _():
            grad_sum.up(j + LAG)

        write_part = jnp.zeros((nstate, BLK), F32)
        read_part = jnp.zeros((nstate, BLK), F32)
        for cols, part_of, inside in cols_of:
            later = last_base[:, cols] * reach[j, :, BLK - 1 :] * arrived[part_of, nstate:, inside]
            carried = later.astype(BF16)
            arrived[part_of, nstate:, inside] = terms[j, :, cols] + later
            carried_all[j, :, cols] = carried
            state = states[j, :, cols] + before[j, :, cols] * arrived[part_of, :nstate, inside]
            write_part = write_part + nt(carried, scaled[rows(j), cols])
            read_part = read_part + nt(state.astype(BF16), weighted[rows(j), cols])
        gpart[j, :nstate] = gpart[j, :nstate] + recip[j] * write_part
        gpart[j, nstate:] = gpart[j, nstate:] + (factor * reach[j]) * read_part
        grad_sum.first(j)
        return carry

    lax.fori_loop(0, nblocks, grad_step, 0)

    def turn_step(k, carry):
        grad_sum.up(LAG - 1 - k)
        grad_sum.meet(final_block - k)
        near(nblocks // 2 + k)
        return carry

    lax.fori_loop(0, LAG, turn_step, 0)
    proj[...] = jnp.zeros_like(proj)

    def proj_step(k, carry):
        j = final_block - k

        @pl.when(k < nblocks - LAG)
        def _():
            grad_sum.meet(j - LAG)

        grad_sum.down(j)
        write_high, write_low = split(grad[j, :nstate])
        read_high, read_low = split(grad[j, nstate:])
        stack = jnp.concatenate([write_high, read_high, write_low, read_low], axis=0)
        for cols, _, _ in cols_of:
            two = nn(stack, out[rows(j), cols])
            proj[:, cols] = proj[:, cols] + (two[:size] + two[size:])
        return carry

    lax.fori_loop(0, nblocks, proj_step, 0)

    for d in range(nc):
        ppart[d] = proj[:, d * width : (d + 1) * width]
    spread = scatters("ctx", nc, c, ppart, pgot, (s7, r7))
    for copy in spread:
        copy.start()

    def far_step(j, carry):
        high = jnp.concatenate([grad[j, :nstate].astype(BF16), grad[j, nstate:].astype(BF16)], axis=0)
        write = short[j, :nstate]
        for cols, _, _ in cols_of:
            value = partial[rows(j), cols] + inverse[:, cols] * tn(write, carried_all[j, :, cols])
            value = value + tn(high, weight[:, cols])
            out[rows(j), cols] = value.astype(BF16)
        return carry

    lax.fori_loop(0, nblocks // 2, far_step, 0)
    acc = ppart[c]
    for k, copy in enumerate(spread):
        copy.wait()
        acc = acc + pgot[k]
    ptotal[c] = acc
    gathered = gathers("ctx", nc, c, ptotal, (s8, r8))
    for copy in gathered:
        copy.start()
    lax.fori_loop(nblocks // 2, nblocks, far_step, 0)

    def drain_step(k, carry):
        coef_sum.drain(k)
        grad_sum.drain(k)
        return carry

    lax.fori_loop(0, nblocks, drain_step, 0)
    for copy in gathered:
        copy.wait()
    for d in range(nc):
        proj_out[:, d * width : (d + 1) * width] = ptotal[d] / (length * nc)


def place_kernel(nblocks, source, proj_source, target, proj_target, sems):
    copies = [
        pltpu.make_async_copy(
            source.at[pl.ds(j * BLK, BLK)], target.at[pl.ds(j * BLK, BLK)], sems.at[j]
        )
        for j in range(nblocks)
    ]
    copies.append(pltpu.make_async_copy(proj_source, proj_target, sems.at[nblocks]))
    for copy in copies:
        copy.start()
    for copy in copies:
        copy.wait()


def local(inner, proj_weight, rates, keep, skip, upstream):
    length, channels = inner.shape
    nstate = proj_weight.shape[0] // 2
    size = 2 * nstate
    nblocks = length // BLK
    factor = 1.0 / nstate**0.5
    nf, nc = lax.axis_size("fsdp"), lax.axis_size("ctx")
    whole = pl.BlockSpec(memory_space=pltpu.VMEM)
    anywhere = pl.BlockSpec(memory_space=pl.ANY)
    shape = jax.ShapeDtypeStruct
    width = channels // nc
    vmem, dma = pltpu.VMEM, pltpu.SemaphoreType.DMA
    entry = (nblocks, nstate, channels)
    half, nq = channels // 2, nc // 2
    chunks = (nblocks, size, BLK)
    line = [vmem(chunks, F32), vmem((2, *chunks), F32), vmem(chunks, F32)]
    line_sems = [dma(chunks[:1]), dma((2, *chunks[:1])), dma(chunks[:1]), dma(chunks[:1])]
    peers = [dma((nc - 1,))] * 2
    scratch = (
        [vmem((size, channels), BF16), vmem((1, length), F32)]
        + [vmem((1, channels), F32)] * 2
        + [vmem((length, channels), BF16)] * 3
        + [vmem((length, channels), F32)]
        + [vmem((BLK, channels), BF16)]
        + [vmem((BLK, channels), F32), vmem((1, channels), F32)]
        + [vmem((nblocks, 1, BLK), F32)] * 2
        + [vmem((nblocks, BLK, BLK), F32)]
        + line + line + [vmem((nblocks, size, BLK), BF16)]
        + [vmem(entry, F32), vmem((nblocks, 1, channels), F32), vmem(entry, F32)]
        + [vmem((1, channels), F32)]
        + [vmem((2, size, half), F32)] * 2
        + [vmem((2, nstate, half), F32), vmem((nq, nstate, half), F32)]
        + [vmem((2, size, half), F32)] * 2
        + [vmem((8, 128), F32), vmem((nc, 8, 128), F32)]
        + [vmem(entry, BF16), vmem((size, channels), F32)]
        + [vmem((nc, size, width), F32), vmem((nc - 1, size, width), F32)]
        + [vmem((nc, size, width), F32)]
        + [dma((4,))] + [dma((nblocks,))] * 2
        + [dma((2,))] * 2
        + peers + line_sems + [dma((nq - 1,))] * 2 + line_sems + peers + peers
    )
    made = pl.pallas_call(
        functools.partial(main_kernel, nstate, factor, nblocks, nf, nc),
        in_specs=[anywhere] * 6,
        out_specs=[whole, whole],
        out_shape=[pltpu.VMEM((length, channels), BF16), pltpu.VMEM((size, channels), F32)],
        scratch_shapes=scratch,
        compiler_params=pltpu.CompilerParams(
            vmem_limit_bytes=55 * 2**20, collective_id=0, has_side_effects=True
        ),
    )(inner, upstream, proj_weight, keep[None], rates[None], skip[None])
    return pl.pallas_call(
        functools.partial(place_kernel, nblocks),
        in_specs=[whole, whole],
        out_specs=[anywhere, anywhere],
        out_shape=[shape((length, channels), BF16), shape((size, channels), F32)],
        scratch_shapes=[dma((nblocks + 1,))],
        compiler_params=pltpu.CompilerParams(vmem_limit_bytes=2**20),
    )(*made)


def solution(mesh):
    placed = (P("ctx", "fsdp"), P(None, "fsdp"), P("fsdp"), P("ctx"), P("fsdp"), P("ctx", "fsdp"))
    return jax.shard_map(
        local,
        mesh=mesh,
        in_specs=placed,
        out_specs=(P("ctx", "fsdp"), P(None, "fsdp")),
        check_vma=False,
    )
```

```python
import functools

import jax
import jax.numpy as jnp
from jax import lax
from jax.experimental import pallas as pl
from jax.experimental.pallas import tpu as pltpu
from jax.sharding import PartitionSpec as P

BLK = 256
LAG = 4
FUSED = 4
AHEAD = 3
MESH = pl.DeviceIdType.MESH
F32 = jnp.float32
BF16 = jnp.bfloat16


def nt(left, right):
    return lax.dot_general(left, right, (((1,), (1,)), ((), ())), preferred_element_type=F32)


def tn(left, right):
    return lax.dot_general(left, right, (((0,), (0,)), ((), ())), preferred_element_type=F32)


def nn(left, right):
    return jnp.dot(left, right, preferred_element_type=F32)


def split(value):
    high = value.astype(BF16)
    return high, (value - high.astype(F32)).astype(BF16)


def pieces(channels):
    half = channels // 2
    width = 512 if half % 512 == 0 else half
    return [
        (slice(at, at + width), at // half, slice(at % half, at % half + width))
        for at in range(0, channels, width)
    ]


def one_minus_exp(x):
    series = 1.0 - x / 9.0
    for k in (8.0, 7.0, 6.0, 5.0, 4.0, 3.0, 2.0):
        series = 1.0 - x / k * series
    return jnp.where(x < 0.25, x * series, 1.0 - jnp.exp(-x))


def copy_to(axis, n, me, k, src, dst, sems):
    return pltpu.make_async_remote_copy(
        src_ref=src,
        dst_ref=dst,
        send_sem=sems[0].at[k - 1],
        recv_sem=sems[1].at[k - 1],
        device_id={axis: lax.rem(me + k, n)},
        device_id_type=MESH,
    )


def scatters(axis, n, me, part, got, sems):
    return [
        copy_to(axis, n, me, k, part.at[lax.rem(me + k, n)], got.at[k - 1], sems)
        for k in range(1, n)
    ]


def gathers(axis, n, me, total, sems):
    own = total.at[me]
    return [copy_to(axis, n, me, k, own, own, sems) for k in range(1, n)]


class LineSum:
    def __init__(self, n, me, part, came, total, up_send, up_recv, down_send, down_recv):
        half = n // 2
        self.part, self.came, self.total = part, came, total
        self.up_send, self.up_recv = up_send, up_recv
        self.down_send, self.down_recv = down_send, down_recv
        left = me < half
        self.depth = jnp.where(left, me, n - 1 - me)
        self.middle = self.depth == half - 1
        self.outermost = self.depth == 0
        self.slot = jnp.where(self.middle, 1, 0)
        self.inward = jnp.where(left, me + 1, me - 1)
        self.outward = jnp.where(left, me - 1, me + 1)

    def rising(self, k, slot):
        return pltpu.make_async_remote_copy(
            src_ref=self.part.at[k], dst_ref=self.came.at[slot, k],
            send_sem=self.up_send.at[k], recv_sem=self.up_recv.at[slot, k],
            device_id={"fsdp": self.inward}, device_id_type=MESH,
        )

    def falling(self, k):
        return pltpu.make_async_remote_copy(
            src_ref=self.total.at[k], dst_ref=self.total.at[k],
            send_sem=self.down_send.at[k], recv_sem=self.down_recv.at[k],
            device_id={"fsdp": self.outward}, device_id_type=MESH,
        )

    def first(self, k):
        @pl.when(self.outermost)
        def _():
            self.rising(k, self.slot).start()

    def up(self, k):
        @pl.when(jnp.logical_not(self.outermost))
        def _():
            self.rising(k, 0).wait_recv()
            self.part[k] = self.part[k] + self.came[0, k]
            self.rising(k, self.slot).start()

    def meet(self, k):
        @pl.when(self.middle)
        def _():
            self.rising(k, 1).wait_recv()
            self.total[k] = self.part[k] + self.came[1, k]

            @pl.when(jnp.logical_not(self.outermost))
            def _():
                self.falling(k).start()

    def down(self, k):
        @pl.when(jnp.logical_not(self.middle))
        def _():
            self.falling(k).wait_recv()

            @pl.when(jnp.logical_not(self.outermost))
            def _():
                self.falling(k).start()

    def drain(self, k):
        self.rising(k, self.slot).wait_send()

        @pl.when(jnp.logical_not(self.outermost))
        def _():
            self.falling(k).wait_send()


def main_kernel(
    nstate, factor, nblocks, nf, nc,
    inner_hbm, upstream_hbm, weight_hbm, keep_hbm, rates_hbm, skip_hbm,
    out, proj_out,
    weight, keep, rates, skip,
    upstream, scaled, weighted, partial, base16, inverse, last_base, reach, recip,
    cross, part, came, coef, gpart, gcame, grad, short,
    states, before, terms, sofar, pack, pairs, chip, chips, leaving, arrived, kept, kept_all,
    carried_all, proj, ppart, pgot, ptotal,
    small_sem, in_sem, up_sem, pair_sems, back_sems, s0, r0, s1, r1, s2, r2, s3, r3, s5, r5, s6, r6, s7, r7, s8, r8,
):
    size = 2 * nstate
    channels = weight.shape[1]
    length = nblocks * BLK
    half = channels // 2
    width = channels // nc
    nq = nc // 2
    fill_width = channels // nblocks
    f = lax.axis_index("fsdp")
    c = lax.axis_index("ctx")
    q, h = c // 2, lax.rem(c, 2)
    other = 1 - h
    cols_of = pieces(channels)
    coef_sum = LineSum(nf, f, part, came, coef, s1, r1, s2, r2)
    grad_sum = LineSum(nf, f, gpart, gcame, grad, s5, r5, s6, r6)

    def rows(j):
        return pl.ds(pl.multiple_of(j * BLK, BLK), BLK)

    def fetch_inner(j):
        return pltpu.make_async_copy(inner_hbm.at[rows(j)], out.at[rows(j)], in_sem.at[j])

    def fetch_upstream(j):
        return pltpu.make_async_copy(upstream_hbm.at[rows(j)], upstream.at[rows(j)], up_sem.at[j])

    def to_partner(src, dst, sems):
        return pltpu.make_async_remote_copy(
            src_ref=src, dst_ref=dst, send_sem=sems.at[0], recv_sem=sems.at[1],
            device_id={"ctx": 2 * q + other}, device_id_type=MESH,
        )

    small = [
        pltpu.make_async_copy(source, target, small_sem.at[i])
        for i, (source, target) in enumerate(
            ((weight_hbm, weight), (keep_hbm, keep), (rates_hbm, rates), (skip_hbm, skip))
        )
    ]
    small[0].start()
    fetch_inner(0).start()
    for copy in small[1:]:
        copy.start()
    for j in range(1, AHEAD):
        fetch_inner(j).start()

    barrier = pltpu.get_barrier_semaphore()
    pl.semaphore_signal(barrier, inc=1, device_id={"fsdp": coef_sum.inward}, device_id_type=MESH)

    @pl.when(jnp.logical_not(coef_sum.outermost))
    def _():
        pl.semaphore_signal(barrier, inc=1, device_id={"fsdp": coef_sum.outward}, device_id_type=MESH)

    for k in range(1, nc):
        pl.semaphore_signal(
            barrier, inc=1, device_id={"ctx": lax.rem(c + k, nc)}, device_id_type=MESH
        )

    def fill(j):
        cols = pl.ds(pl.multiple_of(j * fill_width, fill_width), fill_width)
        rate = rates[:, cols]
        gain = jnp.sqrt(one_minus_exp(2.0 * rate))
        offsets = lax.broadcasted_iota(jnp.int32, (BLK, fill_width), 0).astype(F32) + 1.0
        exponent = offsets * rate
        base16[:, cols] = jnp.exp(-exponent).astype(BF16)
        inverse[:, cols] = gain * jnp.exp(exponent)

    def first_pass(j):
        sums = nt(weight[...], out[rows(j), :])
        part[j, :nstate] = sums[:nstate]
        part[j, nstate:] = sums[nstate:]

    small[0].wait()

    def first_step(j, carry):
        fetch_inner(j).wait()

        @pl.when(j < nblocks - AHEAD)
        def _():
            fetch_inner(j + AHEAD).start()

        @pl.when(j >= nblocks - AHEAD)
        def _():
            fetch_upstream(j - (nblocks - AHEAD)).start()

        first_pass(j)

        @pl.when(j == 0)
        def _():
            pl.semaphore_wait(barrier, nc + jnp.where(coef_sum.outermost, 0, 1))

        coef_sum.first(j)
        return carry

    lax.fori_loop(0, nblocks, first_step, 0)
    for copy in small[1:]:
        copy.wait()
    prod = jnp.concatenate([keep[:, j * BLK : (j + 1) * BLK] for j in range(nblocks)], axis=0)
    lane = lax.broadcasted_iota(jnp.int32, prod.shape, 1)
    shift = 1
    while shift < BLK:
        prod = prod * jnp.where(lane >= shift, pltpu.roll(prod, shift, 1), 1.0)
        shift *= 2
    inverted = 1.0 / prod
    whole_keep = jnp.ones((1, 1), F32)
    for j in range(nblocks):
        reach[j] = prod[j : j + 1]
        recip[j] = inverted[j : j + 1]
        whole_keep = whole_keep * prod[j : j + 1, BLK - 1 :]
    kept[...] = jnp.broadcast_to(whole_keep, kept.shape)
    kept_all[c] = kept[...]
    last_base[...] = jnp.exp(-float(BLK) * rates[...])

    keeps = [
        copy_to("ctx", nc, c, k, kept, kept_all.at[c], (s0, r0)) for k in range(1, nc)
    ]
    for copy in keeps:
        copy.start()

    def fill_step(j, carry):
        fill(j)
        return carry

    lax.fori_loop(0, nblocks, fill_step, 0)

    row = lax.broadcasted_iota(jnp.int32, (BLK, BLK), 0)
    col = lax.broadcasted_iota(jnp.int32, (BLK, BLK), 1)

    def cross_step(j, carry):
        coef_sum.up(j)

        @pl.when(j >= LAG)
        def _():
            coef_sum.meet(j - LAG)

        fetch_upstream(j).wait()

        @pl.when(j < nblocks - AHEAD)
        def _():
            fetch_upstream(j + AHEAD).start()

        total = jnp.zeros((BLK, BLK), F32)
        for cols, _, _ in cols_of:
            w = upstream[rows(j), cols] * base16[:, cols]
            s = (out[rows(j), cols].astype(F32) * inverse[:, cols]).astype(BF16)
            weighted[rows(j), cols] = w
            scaled[rows(j), cols] = s
            total = total + nt(w, s)
        cross[j] = jnp.where(row >= col, total, 0.0)
        return carry

    lax.fori_loop(0, nblocks, cross_step, 0)

    pack[...] = jnp.zeros_like(pack)
    sofar[...] = jnp.ones_like(sofar)

    def state_step(j, carry):
        @pl.when(j < LAG)
        def _():
            coef_sum.meet(nblocks - LAG + j)

        coef_sum.down(j)
        write = (coef[j, :nstate].astype(BF16).astype(F32) * recip[j]).astype(BF16)
        read = (coef[j, nstate:].astype(BF16).astype(F32) * reach[j]).astype(BF16)
        short[j, :nstate] = write
        short[j, nstate:] = read
        for cols, part_of, inside in cols_of:
            decay = last_base[:, cols] * reach[j, :, BLK - 1 :]
            state = pack[part_of, :nstate, inside]
            ahead = sofar[:, cols]
            term = factor * nn(read, weighted[rows(j), cols])
            states[j, :, cols] = state
            before[j, :, cols] = ahead
            terms[j, :, cols] = term
            pack[part_of, :nstate, inside] = decay * (state + nn(write, scaled[rows(j), cols]))
            pack[part_of, nstate:, inside] = pack[part_of, nstate:, inside] + ahead * term
            sofar[:, cols] = ahead * decay
        return carry

    lax.fori_loop(0, nblocks, state_step, 0)
    across = to_partner(pack.at[other], pairs.at[h], pair_sems)
    across.start()
    pairs[h] = pack[h]

    def product_step(j, carry):
        write = coef[j, :nstate] * recip[j]
        read = coef[j, nstate:] * reach[j]
        high, low = split(cross[j])
        two = jnp.concatenate(split(read), axis=0)
        sums = nn(two, high)
        gpart[j, :nstate] = (factor * recip[j]) * (
            sums[:nstate] + (sums[nstate:] + nn(two[:nstate], low))
        )
        two = jnp.concatenate(split(write), axis=0)
        sums = nt(two, high)
        gpart[j, nstate:] = (factor * reach[j]) * (
            sums[:nstate] + (sums[nstate:] + nt(two[:nstate], low))
        )
        return carry

    def near(j):
        turned = jnp.where(
            col >= row, factor * tn(short[j, :nstate], short[j, nstate:]), 0.0
        ).astype(BF16)
        for cols, _, _ in cols_of:
            mixed = nn(turned, weighted[rows(j), cols])
            partial[rows(j), cols] = inverse[:, cols] * mixed + skip[:, cols] * upstream[
                rows(j), cols
            ].astype(F32)

    def near_step(j, carry):
        near(j)
        return carry

    lax.fori_loop(0, nblocks // 4, product_step, 0)
    for copy in keeps:
        copy.wait()
    across.wait()
    span = jnp.exp(-float(length) * rates[:, pl.ds(pl.multiple_of(h * half, half), half)])

    def decay_of(device):
        return span * kept_all[device, :1, :1]

    decay0, decay1 = decay_of(2 * q), decay_of(2 * q + 1)
    chip[0] = pairs[1, :nstate] + decay1 * pairs[0, :nstate]
    chip[1] = pairs[0, nstate:] + decay0 * pairs[1, nstate:]
    there = []
    for k in range(1, nq):
        peer = lax.rem(q + k, nq)
        there.append(
            pltpu.make_async_remote_copy(
                src_ref=chip.at[jnp.where(peer > q, 0, 1)], dst_ref=chips.at[q],
                send_sem=s3.at[k - 1], recv_sem=r3.at[k - 1],
                device_id={"ctx": 2 * peer + h}, device_id_type=MESH,
            )
        )
    for copy in there:
        copy.start()
    lax.fori_loop(nblocks // 4, nblocks, product_step, 0)
    lax.fori_loop(0, nblocks // 2 - 1, near_step, 0)
    for copy in there:
        copy.wait()

    def chip_decay(k):
        return decay_of(2 * k) * decay_of(2 * k + 1)

    zero = jnp.zeros((nstate, half), F32)
    state = lax.fori_loop(0, q, lambda k, state: chips[k] + chip_decay(k) * state, zero)
    later = lax.fori_loop(
        0, nq - 1 - q, lambda k, later: chips[nq - 1 - k] + chip_decay(nq - 1 - k) * later, zero
    )
    leaving[0, :nstate] = state
    leaving[0, nstate:] = pairs[1, nstate:] + decay1 * later
    leaving[1, :nstate] = pairs[0, :nstate] + decay0 * state
    leaving[1, nstate:] = later
    home = to_partner(leaving.at[other], arrived.at[h], back_sems)
    home.start()
    arrived[h] = leaving[h]
    near(nblocks // 2 - 1)
    home.wait()

    final_block = nblocks - 1

    def grad_step(k, carry):
        j = final_block - k

        @pl.when(k >= LAG)
        def _():
            grad_sum.up(j + LAG)

        write_part = jnp.zeros((nstate, BLK), F32)
        read_part = jnp.zeros((nstate, BLK), F32)
        for cols, part_of, inside in cols_of:
            later = last_base[:, cols] * reach[j, :, BLK - 1 :] * arrived[part_of, nstate:, inside]
            carried = later.astype(BF16)
            arrived[part_of, nstate:, inside] = terms[j, :, cols] + later
            carried_all[j, :, cols] = carried
            state = states[j, :, cols] + before[j, :, cols] * arrived[part_of, :nstate, inside]
            write_part = write_part + nt(carried, scaled[rows(j), cols])
            read_part = read_part + nt(state.astype(BF16), weighted[rows(j), cols])
        gpart[j, :nstate] = gpart[j, :nstate] + recip[j] * write_part
        gpart[j, nstate:] = gpart[j, nstate:] + (factor * reach[j]) * read_part
        grad_sum.first(j)
        return carry

    lax.fori_loop(0, nblocks, grad_step, 0)

    def turn_step(k, carry):
        grad_sum.up(LAG - 1 - k)
        grad_sum.meet(final_block - k)
        return carry

    lax.fori_loop(0, LAG, turn_step, 0)
    proj[...] = jnp.zeros_like(proj)

    def proj_step(k, carry):
        j = final_block - k

        @pl.when(k < nblocks - LAG)
        def _():
            grad_sum.meet(j - LAG)

        grad_sum.down(j)
        write_high, write_low = split(grad[j, :nstate])
        read_high, read_low = split(grad[j, nstate:])
        stack = jnp.concatenate([write_high, read_high, write_low, read_low], axis=0)
        for cols, _, _ in cols_of:
            two = nn(stack, out[rows(j), cols])
            proj[:, cols] = proj[:, cols] + (two[:size] + two[size:])
        return carry

    lax.fori_loop(0, nblocks, proj_step, 0)

    for d in range(nc):
        ppart[d] = proj[:, d * width : (d + 1) * width]
    spread = scatters("ctx", nc, c, ppart, pgot, (s7, r7))
    for copy in spread:
        copy.start()

    def far_step(j, carry):
        high = jnp.concatenate([grad[j, :nstate].astype(BF16), grad[j, nstate:].astype(BF16)], axis=0)
        write = short[j, :nstate]
        for cols, _, _ in cols_of:
            value = partial[rows(j), cols] + inverse[:, cols] * tn(write, carried_all[j, :, cols])
            value = value + tn(high, weight[:, cols])
            out[rows(j), cols] = value.astype(BF16)
        return carry

    def end_step(j, carry):
        turned = jnp.where(
            col >= row, factor * tn(short[j, :nstate], short[j, nstate:]), 0.0
        ).astype(BF16)
        high = grad[j].astype(BF16)
        write = short[j, :nstate]
        for cols, _, _ in cols_of:
            mixed = nn(turned, weighted[rows(j), cols]) + tn(write, carried_all[j, :, cols])
            value = inverse[:, cols] * mixed + skip[:, cols] * upstream[rows(j), cols].astype(F32)
            value = value + tn(high, weight[:, cols])
            out[rows(j), cols] = value.astype(BF16)
        return carry

    lax.fori_loop(0, nblocks // 2, far_step, 0)
    acc = ppart[c]
    for k, copy in enumerate(spread):
        copy.wait()
        acc = acc + pgot[k]
    ptotal[c] = acc
    gathered = gathers("ctx", nc, c, ptotal, (s8, r8))
    for copy in gathered:
        copy.start()
    lax.fori_loop(nblocks // 2, nblocks, end_step, 0)

    def drain_step(k, carry):
        coef_sum.drain(k)
        grad_sum.drain(k)
        return carry

    lax.fori_loop(0, nblocks, drain_step, 0)
    for copy in gathered:
        copy.wait()
    for d in range(nc):
        proj_out[:, d * width : (d + 1) * width] = ptotal[d] / (length * nc)


def place_kernel(nblocks, source, proj_source, target, proj_target, sems):
    copies = [
        pltpu.make_async_copy(
            source.at[pl.ds(j * BLK, BLK)], target.at[pl.ds(j * BLK, BLK)], sems.at[j]
        )
        for j in range(nblocks)
    ]
    copies.append(pltpu.make_async_copy(proj_source, proj_target, sems.at[nblocks]))
    for copy in copies:
        copy.start()
    for copy in copies:
        copy.wait()


def local(inner, proj_weight, rates, keep, skip, upstream):
    length, channels = inner.shape
    nstate = proj_weight.shape[0] // 2
    size = 2 * nstate
    nblocks = length // BLK
    factor = 1.0 / nstate**0.5
    nf, nc = lax.axis_size("fsdp"), lax.axis_size("ctx")
    whole = pl.BlockSpec(memory_space=pltpu.VMEM)
    anywhere = pl.BlockSpec(memory_space=pl.ANY)
    shape = jax.ShapeDtypeStruct
    width = channels // nc
    vmem, dma = pltpu.VMEM, pltpu.SemaphoreType.DMA
    entry = (nblocks, nstate, channels)
    half, nq = channels // 2, nc // 2
    chunks = (nblocks, size, BLK)
    line = [vmem(chunks, F32), vmem((2, *chunks), F32), vmem(chunks, F32)]
    line_sems = [dma(chunks[:1]), dma((2, *chunks[:1])), dma(chunks[:1]), dma(chunks[:1])]
    peers = [dma((nc - 1,))] * 2
    scratch = (
        [vmem((size, channels), BF16), vmem((1, length), F32)]
        + [vmem((1, channels), F32)] * 2
        + [vmem((length, channels), BF16)] * 3
        + [vmem((length, channels), F32)]
        + [vmem((BLK, channels), BF16)]
        + [vmem((BLK, channels), F32), vmem((1, channels), F32)]
        + [vmem((nblocks, 1, BLK), F32)] * 2
        + [vmem((nblocks, BLK, BLK), F32)]
        + line + line + [vmem((nblocks, size, BLK), BF16)]
        + [vmem(entry, F32), vmem((nblocks, 1, channels), F32), vmem(entry, F32)]
        + [vmem((1, channels), F32)]
        + [vmem((2, size, half), F32)] * 2
        + [vmem((2, nstate, half), F32), vmem((nq, nstate, half), F32)]
        + [vmem((2, size, half), F32)] * 2
        + [vmem((8, 128), F32), vmem((nc, 8, 128), F32)]
        + [vmem(entry, BF16), vmem((size, channels), F32)]
        + [vmem((nc, size, width), F32), vmem((nc - 1, size, width), F32)]
        + [vmem((nc, size, width), F32)]
        + [dma((4,))] + [dma((nblocks,))] * 2
        + [dma((2,))] * 2
        + peers + line_sems + [dma((nq - 1,))] * 2 + line_sems + peers + peers
    )
    made = pl.pallas_call(
        functools.partial(main_kernel, nstate, factor, nblocks, nf, nc),
        in_specs=[anywhere] * 6,
        out_specs=[whole, whole],
        out_shape=[pltpu.VMEM((length, channels), BF16), pltpu.VMEM((size, channels), F32)],
        scratch_shapes=scratch,
        compiler_params=pltpu.CompilerParams(
            vmem_limit_bytes=55 * 2**20, collective_id=0, has_side_effects=True
        ),
    )(inner, upstream, proj_weight, keep[None], rates[None], skip[None])
    return pl.pallas_call(
        functools.partial(place_kernel, nblocks),
        in_specs=[whole, whole],
        out_specs=[anywhere, anywhere],
        out_shape=[shape((length, channels), BF16), shape((size, channels), F32)],
        scratch_shapes=[dma((nblocks + 1,))],
        compiler_params=pltpu.CompilerParams(vmem_limit_bytes=2**20),
    )(*made)


def solution(mesh):
    placed = (P("ctx", "fsdp"), P(None, "fsdp"), P("fsdp"), P("ctx"), P("fsdp"), P("ctx", "fsdp"))
    return jax.shard_map(
        local,
        mesh=mesh,
        in_specs=placed,
        out_specs=(P("ctx", "fsdp"), P(None, "fsdp")),
        check_vma=False,
    )
```

```python
import functools

import jax
import jax.numpy as jnp
from jax import lax
from jax.experimental import pallas as pl
from jax.experimental.pallas import tpu as pltpu
from jax.sharding import PartitionSpec as P

BLK = 256
LAG = 4
FUSED = 2
AHEAD = 3
MESH = pl.DeviceIdType.MESH
F32 = jnp.float32
BF16 = jnp.bfloat16


def nt(left, right):
    return lax.dot_general(left, right, (((1,), (1,)), ((), ())), preferred_element_type=F32)


def tn(left, right):
    return lax.dot_general(left, right, (((0,), (0,)), ((), ())), preferred_element_type=F32)


def nn(left, right):
    return jnp.dot(left, right, preferred_element_type=F32)


def split(value):
    high = value.astype(BF16)
    return high, (value - high.astype(F32)).astype(BF16)


def pieces(channels):
    half = channels // 2
    width = 512 if half % 512 == 0 else half
    return [
        (slice(at, at + width), at // half, slice(at % half, at % half + width))
        for at in range(0, channels, width)
    ]


def one_minus_exp(x):
    series = 1.0 - x / 9.0
    for k in (8.0, 7.0, 6.0, 5.0, 4.0, 3.0, 2.0):
        series = 1.0 - x / k * series
    return jnp.where(x < 0.25, x * series, 1.0 - jnp.exp(-x))


def copy_to(axis, n, me, k, src, dst, sems):
    return pltpu.make_async_remote_copy(
        src_ref=src,
        dst_ref=dst,
        send_sem=sems[0].at[k - 1],
        recv_sem=sems[1].at[k - 1],
        device_id={axis: lax.rem(me + k, n)},
        device_id_type=MESH,
    )


def scatters(axis, n, me, part, got, sems):
    return [
        copy_to(axis, n, me, k, part.at[lax.rem(me + k, n)], got.at[k - 1], sems)
        for k in range(1, n)
    ]


def gathers(axis, n, me, total, sems):
    own = total.at[me]
    return [copy_to(axis, n, me, k, own, own, sems) for k in range(1, n)]


class LineSum:
    def __init__(self, n, me, part, came, total, up_send, up_recv, down_send, down_recv):
        half = n // 2
        self.part, self.came, self.total = part, came, total
        self.up_send, self.up_recv = up_send, up_recv
        self.down_send, self.down_recv = down_send, down_recv
        left = me < half
        self.depth = jnp.where(left, me, n - 1 - me)
        self.middle = self.depth == half - 1
        self.outermost = self.depth == 0
        self.slot = jnp.where(self.middle, 1, 0)
        self.inward = jnp.where(left, me + 1, me - 1)
        self.outward = jnp.where(left, me - 1, me + 1)

    def rising(self, k, slot):
        return pltpu.make_async_remote_copy(
            src_ref=self.part.at[k], dst_ref=self.came.at[slot, k],
            send_sem=self.up_send.at[k], recv_sem=self.up_recv.at[slot, k],
            device_id={"fsdp": self.inward}, device_id_type=MESH,
        )

    def falling(self, k):
        return pltpu.make_async_remote_copy(
            src_ref=self.total.at[k], dst_ref=self.total.at[k],
            send_sem=self.down_send.at[k], recv_sem=self.down_recv.at[k],
            device_id={"fsdp": self.outward}, device_id_type=MESH,
        )

    def first(self, k):
        @pl.when(self.outermost)
        def _():
            self.rising(k, self.slot).start()

    def up(self, k):
        @pl.when(jnp.logical_not(self.outermost))
        def _():
            self.rising(k, 0).wait_recv()
            self.part[k] = self.part[k] + self.came[0, k]
            self.rising(k, self.slot).start()

    def meet(self, k):
        @pl.when(self.middle)
        def _():
            self.rising(k, 1).wait_recv()
            self.total[k] = self.part[k] + self.came[1, k]

            @pl.when(jnp.logical_not(self.outermost))
            def _():
                self.falling(k).start()

    def down(self, k):
        @pl.when(jnp.logical_not(self.middle))
        def _():
            self.falling(k).wait_recv()

            @pl.when(jnp.logical_not(self.outermost))
            def _():
                self.falling(k).start()

    def drain(self, k):
        self.rising(k, self.slot).wait_send()

        @pl.when(jnp.logical_not(self.outermost))
        def _():
            self.falling(k).wait_send()


def main_kernel(
    nstate, factor, nblocks, nf, nc,
    inner_hbm, upstream_hbm, weight_hbm, keep_hbm, rates_hbm, skip_hbm,
    out, proj_out,
    weight, keep, rates, skip,
    upstream, scaled, weighted, partial, base16, inverse, last_base, reach, recip,
    cross, part, came, coef, gpart, gcame, grad, short,
    states, before, terms, sofar, pack, pairs, chip, chips, leaving, arrived, kept, kept_all,
    carried_all, proj, ppart, pgot, ptotal,
    small_sem, in_sem, up_sem, pair_sems, back_sems, s0, r0, s1, r1, s2, r2, s3, r3, s5, r5, s6, r6, s7, r7, s8, r8,
):
    size = 2 * nstate
    channels = weight.shape[1]
    length = nblocks * BLK
    half = channels // 2
    width = channels // nc
    nq = nc // 2
    fill_width = channels // nblocks
    f = lax.axis_index("fsdp")
    c = lax.axis_index("ctx")
    q, h = c // 2, lax.rem(c, 2)
    other = 1 - h
    cols_of = pieces(channels)
    coef_sum = LineSum(nf, f, part, came, coef, s1, r1, s2, r2)
    grad_sum = LineSum(nf, f, gpart, gcame, grad, s5, r5, s6, r6)

    def rows(j):
        return pl.ds(pl.multiple_of(j * BLK, BLK), BLK)

    def fetch_inner(j):
        return pltpu.make_async_copy(inner_hbm.at[rows(j)], out.at[rows(j)], in_sem.at[j])

    def fetch_upstream(j):
        return pltpu.make_async_copy(upstream_hbm.at[rows(j)], upstream.at[rows(j)], up_sem.at[j])

    def to_partner(src, dst, sems):
        return pltpu.make_async_remote_copy(
            src_ref=src, dst_ref=dst, send_sem=sems.at[0], recv_sem=sems.at[1],
            device_id={"ctx": 2 * q + other}, device_id_type=MESH,
        )

    small = [
        pltpu.make_async_copy(source, target, small_sem.at[i])
        for i, (source, target) in enumerate(
            ((weight_hbm, weight), (keep_hbm, keep), (rates_hbm, rates), (skip_hbm, skip))
        )
    ]
    small[0].start()
    fetch_inner(0).start()
    for copy in small[1:]:
        copy.start()
    for j in range(1, AHEAD):
        fetch_inner(j).start()

    barrier = pltpu.get_barrier_semaphore()
    pl.semaphore_signal(barrier, inc=1, device_id={"fsdp": coef_sum.inward}, device_id_type=MESH)

    @pl.when(jnp.logical_not(coef_sum.outermost))
    def _():
        pl.semaphore_signal(barrier, inc=1, device_id={"fsdp": coef_sum.outward}, device_id_type=MESH)

    for k in range(1, nc):
        pl.semaphore_signal(
            barrier, inc=1, device_id={"ctx": lax.rem(c + k, nc)}, device_id_type=MESH
        )

    def fill(j):
        cols = pl.ds(pl.multiple_of(j * fill_width, fill_width), fill_width)
        rate = rates[:, cols]
        gain = jnp.sqrt(one_minus_exp(2.0 * rate))
        offsets = lax.broadcasted_iota(jnp.int32, (BLK, fill_width), 0).astype(F32) + 1.0
        exponent = offsets * rate
        base16[:, cols] = jnp.exp(-exponent).astype(BF16)
        inverse[:, cols] = gain * jnp.exp(exponent)

    def first_pass(j):
        sums = nt(weight[...], out[rows(j), :])
        part[j, :nstate] = sums[:nstate]
        part[j, nstate:] = sums[nstate:]

    small[0].wait()

    def first_step(j, carry):
        fetch_inner(j).wait()

        @pl.when(j < nblocks - AHEAD)
        def _():
            fetch_inner(j + AHEAD).start()

        @pl.when(j >= nblocks - AHEAD)
        def _():
            fetch_upstream(j - (nblocks - AHEAD)).start()

        first_pass(j)

        @pl.when(j == 0)
        def _():
            pl.semaphore_wait(barrier, nc + jnp.where(coef_sum.outermost, 0, 1))

        coef_sum.first(j)
        return carry

    lax.fori_loop(0, nblocks, first_step, 0)
    for copy in small[1:]:
        copy.wait()
    prod = jnp.concatenate([keep[:, j * BLK : (j + 1) * BLK] for j in range(nblocks)], axis=0)
    lane = lax.broadcasted_iota(jnp.int32, prod.shape, 1)
    shift = 1
    while shift < BLK:
        prod = prod * jnp.where(lane >= shift, pltpu.roll(prod, shift, 1), 1.0)
        shift *= 2
    inverted = 1.0 / prod
    whole_keep = jnp.ones((1, 1), F32)
    for j in range(nblocks):
        reach[j] = prod[j : j + 1]
        recip[j] = inverted[j : j + 1]
        whole_keep = whole_keep * prod[j : j + 1, BLK - 1 :]
    kept[...] = jnp.broadcast_to(whole_keep, kept.shape)
    kept_all[c] = kept[...]
    last_base[...] = jnp.exp(-float(BLK) * rates[...])

    keeps = [
        copy_to("ctx", nc, c, k, kept, kept_all.at[c], (s0, r0)) for k in range(1, nc)
    ]
    for copy in keeps:
        copy.start()

    def fill_step(j, carry):
        fill(j)
        return carry

    lax.fori_loop(0, nblocks, fill_step, 0)

    row = lax.broadcasted_iota(jnp.int32, (BLK, BLK), 0)
    col = lax.broadcasted_iota(jnp.int32, (BLK, BLK), 1)

    def cross_step(j, carry):
        coef_sum.up(j)

        @pl.when(j >= LAG)
        def _():
            coef_sum.meet(j - LAG)

        fetch_upstream(j).wait()

        @pl.when(j < nblocks - AHEAD)
        def _():
            fetch_upstream(j + AHEAD).start()

        total = jnp.zeros((BLK, BLK), F32)
        for cols, _, _ in cols_of:
            w = upstream[rows(j), cols] * base16[:, cols]
            s = (out[rows(j), cols].astype(F32) * inverse[:, cols]).astype(BF16)
            weighted[rows(j), cols] = w
            scaled[rows(j), cols] = s
            total = total + nt(w, s)
        cross[j] = jnp.where(row >= col, total, 0.0)
        return carry

    lax.fori_loop(0, nblocks, cross_step, 0)

    pack[...] = jnp.zeros_like(pack)
    sofar[...] = jnp.ones_like(sofar)

    def state_step(j, carry):
        @pl.when(j < LAG)
        def _():
            coef_sum.meet(nblocks - LAG + j)

        coef_sum.down(j)
        write = (coef[j, :nstate].astype(BF16).astype(F32) * recip[j]).astype(BF16)
        read = (coef[j, nstate:].astype(BF16).astype(F32) * reach[j]).astype(BF16)
        short[j, :nstate] = write
        short[j, nstate:] = read
        for cols, part_of, inside in cols_of:
            decay = last_base[:, cols] * reach[j, :, BLK - 1 :]
            state = pack[part_of, :nstate, inside]
            ahead = sofar[:, cols]
            term = factor * nn(read, weighted[rows(j), cols])
            states[j, :, cols] = state
            before[j, :, cols] = ahead
            terms[j, :, cols] = term
            pack[part_of, :nstate, inside] = decay * (state + nn(write, scaled[rows(j), cols]))
            pack[part_of, nstate:, inside] = pack[part_of, nstate:, inside] + ahead * term
            sofar[:, cols] = ahead * decay
        return carry

    lax.fori_loop(0, nblocks, state_step, 0)
    across = to_partner(pack.at[other], pairs.at[h], pair_sems)
    across.start()
    pairs[h] = pack[h]

    def product_step(j, carry):
        write = coef[j, :nstate] * recip[j]
        read = coef[j, nstate:] * reach[j]
        high, low = split(cross[j])
        two = jnp.concatenate(split(read), axis=0)
        sums = nn(two, high)
        gpart[j, :nstate] = (factor * recip[j]) * (
            sums[:nstate] + (sums[nstate:] + nn(two[:nstate], low))
        )
        two = jnp.concatenate(split(write), axis=0)
        sums = nt(two, high)
        gpart[j, nstate:] = (factor * reach[j]) * (
            sums[:nstate] + (sums[nstate:] + nt(two[:nstate], low))
        )
        return carry

    def near(j):
        turned = jnp.where(
            col >= row, factor * tn(short[j, :nstate], short[j, nstate:]), 0.0
        ).astype(BF16)
        for cols, _, _ in cols_of:
            mixed = nn(turned, weighted[rows(j), cols])
            partial[rows(j), cols] = inverse[:, cols] * mixed + skip[:, cols] * upstream[
                rows(j), cols
            ].astype(F32)

    def near_step(j, carry):
        near(j)
        return carry

    lax.fori_loop(0, nblocks // 4, product_step, 0)
    for copy in keeps:
        copy.wait()
    across.wait()
    span = jnp.exp(-float(length) * rates[:, pl.ds(pl.multiple_of(h * half, half), half)])

    def decay_of(device):
        return span * kept_all[device, :1, :1]

    decay0, decay1 = decay_of(2 * q), decay_of(2 * q + 1)
    chip[0] = pairs[1, :nstate] + decay1 * pairs[0, :nstate]
    chip[1] = pairs[0, nstate:] + decay0 * pairs[1, nstate:]
    there = []
    for k in range(1, nq):
        peer = lax.rem(q + k, nq)
        there.append(
            pltpu.make_async_remote_copy(
                src_ref=chip.at[jnp.where(peer > q, 0, 1)], dst_ref=chips.at[q],
                send_sem=s3.at[k - 1], recv_sem=r3.at[k - 1],
                device_id={"ctx": 2 * peer + h}, device_id_type=MESH,
            )
        )
    for copy in there:
        copy.start()
    lax.fori_loop(nblocks // 4, nblocks, product_step, 0)
    lax.fori_loop(0, nblocks // 2 - 1, near_step, 0)
    for copy in there:
        copy.wait()

    def chip_decay(k):
        return decay_of(2 * k) * decay_of(2 * k + 1)

    zero = jnp.zeros((nstate, half), F32)
    state = lax.fori_loop(0, q, lambda k, state: chips[k] + chip_decay(k) * state, zero)
    later = lax.fori_loop(
        0, nq - 1 - q, lambda k, later: chips[nq - 1 - k] + chip_decay(nq - 1 - k) * later, zero
    )
    leaving[0, :nstate] = state
    leaving[0, nstate:] = pairs[1, nstate:] + decay1 * later
    leaving[1, :nstate] = pairs[0, :nstate] + decay0 * state
    leaving[1, nstate:] = later
    home = to_partner(leaving.at[other], arrived.at[h], back_sems)
    home.start()
    arrived[h] = leaving[h]
    near(nblocks // 2 - 1)
    home.wait()

    final_block = nblocks - 1

    def grad_step(k, carry):
        j = final_block - k

        @pl.when(k >= LAG)
        def _():
            grad_sum.up(j + LAG)

        write_part = jnp.zeros((nstate, BLK), F32)
        read_part = jnp.zeros((nstate, BLK), F32)
        for cols, part_of, inside in cols_of:
            later = last_base[:, cols] * reach[j, :, BLK - 1 :] * arrived[part_of, nstate:, inside]
            carried = later.astype(BF16)
            arrived[part_of, nstate:, inside] = terms[j, :, cols] + later
            carried_all[j, :, cols] = carried
            state = states[j, :, cols] + before[j, :, cols] * arrived[part_of, :nstate, inside]
            write_part = write_part + nt(carried, scaled[rows(j), cols])
            read_part = read_part + nt(state.astype(BF16), weighted[rows(j), cols])
        gpart[j, :nstate] = gpart[j, :nstate] + recip[j] * write_part
        gpart[j, nstate:] = gpart[j, nstate:] + (factor * reach[j]) * read_part
        grad_sum.first(j)
        return carry

    lax.fori_loop(0, nblocks, grad_step, 0)

    def turn_step(k, carry):
        grad_sum.up(LAG - 1 - k)
        grad_sum.meet(final_block - k)

        @pl.when(k < LAG - FUSED)
        def _():
            near(nblocks // 2 + k)

        return carry

    lax.fori_loop(0, LAG, turn_step, 0)
    proj[...] = jnp.zeros_like(proj)

    def proj_step(k, carry):
        j = final_block - k

        @pl.when(k < nblocks - LAG)
        def _():
            grad_sum.meet(j - LAG)

        grad_sum.down(j)
        write_high, write_low = split(grad[j, :nstate])
        read_high, read_low = split(grad[j, nstate:])
        stack = jnp.concatenate([write_high, read_high, write_low, read_low], axis=0)
        for cols, _, _ in cols_of:
            two = nn(stack, out[rows(j), cols])
            proj[:, cols] = proj[:, cols] + (two[:size] + two[size:])
        return carry

    lax.fori_loop(0, nblocks, proj_step, 0)

    for d in range(nc):
        ppart[d] = proj[:, d * width : (d + 1) * width]
    spread = scatters("ctx", nc, c, ppart, pgot, (s7, r7))
    for copy in spread:
        copy.start()

    def far_step(j, carry):
        high = jnp.concatenate([grad[j, :nstate].astype(BF16), grad[j, nstate:].astype(BF16)], axis=0)
        write = short[j, :nstate]
        for cols, _, _ in cols_of:
            value = partial[rows(j), cols] + inverse[:, cols] * tn(write, carried_all[j, :, cols])
            value = value + tn(high, weight[:, cols])
            out[rows(j), cols] = value.astype(BF16)
        return carry

    def end_step(j, carry):
        turned = jnp.where(
            col >= row, factor * tn(short[j, :nstate], short[j, nstate:]), 0.0
        ).astype(BF16)
        high = grad[j].astype(BF16)
        write = short[j, :nstate]
        for cols, _, _ in cols_of:
            mixed = nn(turned, weighted[rows(j), cols]) + tn(write, carried_all[j, :, cols])
            value = inverse[:, cols] * mixed + skip[:, cols] * upstream[rows(j), cols].astype(F32)
            value = value + tn(high, weight[:, cols])
            out[rows(j), cols] = value.astype(BF16)
        return carry

    lax.fori_loop(0, nblocks // 2, far_step, 0)
    acc = ppart[c]
    for k, copy in enumerate(spread):
        copy.wait()
        acc = acc + pgot[k]
    ptotal[c] = acc
    gathered = gathers("ctx", nc, c, ptotal, (s8, r8))
    for copy in gathered:
        copy.start()
    lax.fori_loop(nblocks // 2, nblocks - FUSED, far_step, 0)
    lax.fori_loop(nblocks - FUSED, nblocks, end_step, 0)

    def drain_step(k, carry):
        coef_sum.drain(k)
        grad_sum.drain(k)
        return carry

    lax.fori_loop(0, nblocks, drain_step, 0)
    for copy in gathered:
        copy.wait()
    for d in range(nc):
        proj_out[:, d * width : (d + 1) * width] = ptotal[d] / (length * nc)


def place_kernel(nblocks, source, proj_source, target, proj_target, sems):
    copies = [
        pltpu.make_async_copy(
            source.at[pl.ds(j * BLK, BLK)], target.at[pl.ds(j * BLK, BLK)], sems.at[j]
        )
        for j in range(nblocks)
    ]
    copies.append(pltpu.make_async_copy(proj_source, proj_target, sems.at[nblocks]))
    for copy in copies:
        copy.start()
    for copy in copies:
        copy.wait()


def local(inner, proj_weight, rates, keep, skip, upstream):
    length, channels = inner.shape
    nstate = proj_weight.shape[0] // 2
    size = 2 * nstate
    nblocks = length // BLK
    factor = 1.0 / nstate**0.5
    nf, nc = lax.axis_size("fsdp"), lax.axis_size("ctx")
    whole = pl.BlockSpec(memory_space=pltpu.VMEM)
    anywhere = pl.BlockSpec(memory_space=pl.ANY)
    shape = jax.ShapeDtypeStruct
    width = channels // nc
    vmem, dma = pltpu.VMEM, pltpu.SemaphoreType.DMA
    entry = (nblocks, nstate, channels)
    half, nq = channels // 2, nc // 2
    chunks = (nblocks, size, BLK)
    line = [vmem(chunks, F32), vmem((2, *chunks), F32), vmem(chunks, F32)]
    line_sems = [dma(chunks[:1]), dma((2, *chunks[:1])), dma(chunks[:1]), dma(chunks[:1])]
    peers = [dma((nc - 1,))] * 2
    scratch = (
        [vmem((size, channels), BF16), vmem((1, length), F32)]
        + [vmem((1, channels), F32)] * 2
        + [vmem((length, channels), BF16)] * 3
        + [vmem((length, channels), F32)]
        + [vmem((BLK, channels), BF16)]
        + [vmem((BLK, channels), F32), vmem((1, channels), F32)]
        + [vmem((nblocks, 1, BLK), F32)] * 2
        + [vmem((nblocks, BLK, BLK), F32)]
        + line + line + [vmem((nblocks, size, BLK), BF16)]
        + [vmem(entry, F32), vmem((nblocks, 1, channels), F32), vmem(entry, F32)]
        + [vmem((1, channels), F32)]
        + [vmem((2, size, half), F32)] * 2
        + [vmem((2, nstate, half), F32), vmem((nq, nstate, half), F32)]
        + [vmem((2, size, half), F32)] * 2
        + [vmem((8, 128), F32), vmem((nc, 8, 128), F32)]
        + [vmem(entry, BF16), vmem((size, channels), F32)]
        + [vmem((nc, size, width), F32), vmem((nc - 1, size, width), F32)]
        + [vmem((nc, size, width), F32)]
        + [dma((4,))] + [dma((nblocks,))] * 2
        + [dma((2,))] * 2
        + peers + line_sems + [dma((nq - 1,))] * 2 + line_sems + peers + peers
    )
    made = pl.pallas_call(
        functools.partial(main_kernel, nstate, factor, nblocks, nf, nc),
        in_specs=[anywhere] * 6,
        out_specs=[whole, whole],
        out_shape=[pltpu.VMEM((length, channels), BF16), pltpu.VMEM((size, channels), F32)],
        scratch_shapes=scratch,
        compiler_params=pltpu.CompilerParams(
            vmem_limit_bytes=55 * 2**20, collective_id=0, has_side_effects=True
        ),
    )(inner, upstream, proj_weight, keep[None], rates[None], skip[None])
    return pl.pallas_call(
        functools.partial(place_kernel, nblocks),
        in_specs=[whole, whole],
        out_specs=[anywhere, anywhere],
        out_shape=[shape((length, channels), BF16), shape((size, channels), F32)],
        scratch_shapes=[dma((nblocks + 1,))],
        compiler_params=pltpu.CompilerParams(vmem_limit_bytes=2**20),
    )(*made)


def solution(mesh):
    placed = (P("ctx", "fsdp"), P(None, "fsdp"), P("fsdp"), P("ctx"), P("fsdp"), P("ctx", "fsdp"))
    return jax.shard_map(
        local,
        mesh=mesh,
        in_specs=placed,
        out_specs=(P("ctx", "fsdp"), P(None, "fsdp")),
        check_vma=False,
    )
```
